32 devices in a mesh: seq: 2 (over core), batch: 16 (over z, y, x).
Axes of the slice: x: 2, y: 2, z: 4, core: 2. Of those that a mesh axis runs over, the one named last changes fastest.
Arguments:
- tokens: bfloat16 [16, 512, 768], P('batch', 'seq'), may hold values from -6 to 6
- w_qkv: bfloat16 [768, 2304], P('seq'), may hold values from -0.21875 to 0.21875
- q_bias: float32 [768], replicated, may hold values from -3 to 3
- v_bias: float32 [768], replicated, may hold values from -3 to 3
- w_out: bfloat16 [768, 768], P('seq'), may hold values from -1.75 to 1.75
- out_bias: float32 [768], replicated, may hold values from -2 to 2
- attn_gain: float32 [768], replicated, may hold values from 0.1 to 1.9
- attn_shift: float32 [768], replicated, may hold values from -2 to 2
- w_up: bfloat16 [768, 3072], P('seq'), may hold values from -0.21875 to 0.21875
- up_bias: float32 [3072], replicated, may hold values from -3 to 3
- w_down: bfloat16 [3072, 768], P('seq'), may hold values from -0.109375 to 0.109375
- down_bias: float32 [768], replicated, may hold values from -2 to 2
- ffn_gain: float32 [768], replicated, may hold values from 0.1 to 1.9
- ffn_shift: float32 [768], replicated, may hold values from -2 to 2
- seq_len: int32 [16], P('batch'), may hold values from 256 to 512, as said below
- grad_pos: int32 [16, 80], P('batch'), may hold values from 0 to 511, as said below
- grad_count: int32 [16], P('batch'), may hold values from 10 to 80, as said below
- out_grad: bfloat16 [16, 80, 768], P('batch'), may hold values from -6 to 6
Outputs:
- output: bfloat16 [16, 512, 768], P('batch', 'seq')
- grad_tokens: bfloat16 [16, 512, 768], P('batch', 'seq')
- grad_w_qkv: float32 [768, 2304], P('seq')
- grad_q_bias: float32 [768], P('seq')
- grad_v_bias: float32 [768], P('seq')
- grad_w_out: float32 [768, 768], P('seq')
- grad_out_bias: float32 [768], P('seq')
- grad_attn_gain: float32 [768], P('seq')
- grad_attn_shift: float32 [768], P('seq')
- grad_w_up: float32 [768, 3072], P('seq')
- grad_up_bias: float32 [3072], P('seq')
- grad_w_down: float32 [3072, 768], P('seq')
- grad_down_bias: float32 [768], P('seq')
- grad_ffn_gain: float32 [768], P('seq')
- grad_ffn_shift: float32 [768], P('seq')
The draws below stay inside these ranges and needn't reach their ends.
Inputs may be any that keep to these rules, and one draw needn't show every extreme that they name: `seq_len`: 512 is reached by some sequence in every draw. `grad_count`: 80 is reached by some sequence in every draw. `grad_pos`: the entries of one sequence are distinct and lie below its seq_len; entries at or past grad_count are not used.
All inputs are finite; a program needn't handle non-finite values.
Results may differ from the reference program's by a relative error of at most 0.015.
Values may be sent and summed in bfloat16 or wider, within the bound.
A program may use at most 192 MiB of HBM per device.

```python
import jax
import jax.numpy as jnp
from jax import lax

D = 768
FF = 3072
HEADS = 12
HEAD_DIM = 64
LEN = 512
PMAX = 80
SEQUENCES = 16


def common_draw(key):
    base_key = jax.random.fold_in(key, 17)
    key_len, key_pick, key_scale, key_jitter, key_perm, key_full = jax.random.split(base_key, 6)
    seq_index = jnp.arange(SEQUENCES, dtype=jnp.int32)
    lengths = jax.random.randint(key_len, (SEQUENCES,), LEN // 2, LEN + 1, dtype=jnp.int32)
    longest = jax.random.randint(key_pick, (), 0, SEQUENCES, dtype=jnp.int32)
    lengths = jnp.where(seq_index == longest, LEN, lengths).astype(jnp.int32)
    base_count = max(PMAX // 8, 1)
    exponent = jax.random.randint(key_scale, (SEQUENCES,), 0, 4, dtype=jnp.int32)
    floor_count = base_count * jnp.left_shift(jnp.ones_like(exponent), exponent)
    jitter = jax.random.randint(key_jitter, (SEQUENCES,), 0, PMAX, dtype=jnp.int32)
    counts = jnp.minimum(PMAX, floor_count + jitter % floor_count)
    fullest = jax.random.randint(key_full, (), 0, SEQUENCES, dtype=jnp.int32)
    counts = jnp.where(seq_index == fullest, PMAX, counts).astype(jnp.int32)
    perm_keys = jax.random.split(key_perm, SEQUENCES)
    shuffled = jax.vmap(lambda one_key: jax.random.permutation(one_key, LEN))(perm_keys).astype(jnp.int32)
    outside = (shuffled >= lengths[:, None]).astype(jnp.int32)
    sort_order = jnp.argsort(outside, axis=1, stable=True)
    positions = jnp.take_along_axis(shuffled, sort_order, axis=1)[:, :PMAX].astype(jnp.int32)
    return (lengths, positions, counts)


def draw_seq_len(key, part):
    return common_draw(key)[0]


def draw_grad_pos(key, part):
    return common_draw(key)[1]


def draw_grad_count(key, part):
    return common_draw(key)[2]


def level_of(key, dims, shards, low, largest):
    def one(dim, parts):
        draws = jax.random.uniform(jax.random.fold_in(jax.random.fold_in(key, 6), dim), (parts,), jnp.float32, low / len(shards), largest / len(shards))
        return jnp.repeat(jnp.exp(draws), dims[dim] // parts).reshape((-1,) + (1,) * (len(dims) - dim - 1))

    gain = one(*shards[0])
    for cut in shards[1:]:
        gain = gain * one(*cut)
    return gain


def gaussian(key, shape, scale, bound, pieces=(), kind=jnp.bfloat16):
    values = scale * jax.random.normal(key, shape, jnp.float32)
    if pieces:
        values = values * level_of(key, shape, pieces, -0.22, 0.18)
    return jnp.clip(values, -bound, bound).astype(kind)


def setup_inputs(seed: int = 0) -> dict:
    splits = jax.random.split(jax.random.key(seed), 19)
    tokens = gaussian(splits[0], (SEQUENCES, LEN, D), 1.0, 6.0, ((0, 16), (1, 2)))
    w_qkv = gaussian(splits[1], (D, 3 * D), D ** -0.5, 0.21875, ((0, 2),))
    q_bias = gaussian(splits[2], (D,), 0.5, 3.0, (), jnp.float32)
    v_bias = gaussian(splits[3], (D,), 0.5, 3.0, (), jnp.float32)
    w_out = gaussian(splits[4], (D, D), (D // 64) ** -0.5, 1.75, ((0, 2),))
    out_bias = gaussian(splits[5], (D,), 0.3, 2.0, (), jnp.float32)
    attn_gain = jnp.clip(1.0 + 0.18 * jax.random.normal(splits[6], (D,), jnp.float32), 0.1, 1.9)
    attn_shift = gaussian(splits[7], (D,), 0.3, 2.0, (), jnp.float32)
    w_up = gaussian(splits[8], (D, FF), D ** -0.5, 0.21875, ((0, 2),))
    up_bias = gaussian(splits[9], (FF,), 0.5, 3.0, (), jnp.float32)
    w_down = gaussian(splits[10], (FF, D), FF ** -0.5, 0.109375, ((0, 2),))
    down_bias = gaussian(splits[11], (D,), 0.3, 2.0, (), jnp.float32)
    ffn_gain = jnp.clip(1.0 + 0.18 * jax.random.normal(splits[12], (D,), jnp.float32), 0.1, 1.9)
    ffn_shift = gaussian(splits[13], (D,), 0.3, 2.0, (), jnp.float32)
    seq_len = draw_seq_len(jax.random.fold_in(splits[18], 71), 0)
    grad_pos = draw_grad_pos(jax.random.fold_in(splits[18], 71), 0)
    grad_count = draw_grad_count(jax.random.fold_in(splits[18], 71), 0)
    out_grad = gaussian(splits[17], (SEQUENCES, PMAX, D), 1.0, 6.0, ((0, 16),))
    return dict(tokens=tokens, w_qkv=w_qkv, q_bias=q_bias, v_bias=v_bias, w_out=w_out, out_bias=out_bias, attn_gain=attn_gain, attn_shift=attn_shift, w_up=w_up, up_bias=up_bias, w_down=w_down, down_bias=down_bias, ffn_gain=ffn_gain, ffn_shift=ffn_shift, seq_len=seq_len, grad_pos=grad_pos, grad_count=grad_count, out_grad=out_grad)


@jax.custom_vjp
def low(v):
    return lax.optimization_barrier(v.astype(jnp.bfloat16)).astype(jnp.float32)

@jax.custom_vjp
def low_back(v):
    return v

def low_keep(v):
    return (low(v), None)

def low_pass(kept, grad):
    return (grad,)

def back_keep(v):
    return (v, None)

def back_low(kept, grad):
    return (low(grad),)
low.defvjp(low_keep, low_pass)
low_back.defvjp(back_keep, back_low)
masked_fill = -1000000000.0
norm_eps = 1e-05
highest = lax.Precision.HIGHEST

def layer_norm(hidden, gain_vec, offset):
    center = hidden - lax.optimization_barrier(jnp.mean(hidden, axis=-1, keepdims=True))
    spread = lax.optimization_barrier(jnp.mean(center * center, axis=-1, keepdims=True))
    return center * lax.rsqrt(spread + norm_eps) * gain_vec + offset

def matmul(left_in, right_in):
    return jnp.dot(left_in, right_in, precision=highest)

def forward(params, tokens, length):
    w_qkv, q_bias, v_bias, w_out, out_bias, attn_gain, attn_shift, w_up, up_bias, w_down, down_bias, ffn_gain, ffn_shift = params
    score_scale = HEAD_DIM ** (-0.5)
    packed = matmul(tokens, w_qkv) + jnp.concatenate([q_bias, jnp.zeros_like(q_bias), v_bias])
    packed = low_back(low(packed)).reshape(LEN, 3, HEADS, HEAD_DIM)

    def attend(head_block):
        queries = head_block[:, 0]
        key_rows = head_block[:, 1]
        values = head_block[:, 2]
        scores = jnp.einsum('qhd,khd->hqk', queries, key_rows, precision=highest) * score_scale
        scores = low_back(scores)
        key_valid = jnp.arange(LEN) < length
        scores = jnp.where(key_valid[None, None, :], scores, masked_fill)
        attn_probs = low(jax.nn.softmax(scores, axis=-1))
        mixed = jnp.einsum('hqk,khd->qhd', attn_probs, values, precision=highest)
        return mixed.reshape(LEN, D)
    context = low_back(low(jax.checkpoint(attend)(packed)))
    attn_out = low_back(matmul(context, w_out) + out_bias)
    normed = layer_norm(tokens + attn_out, attn_gain, attn_shift)
    up_proj = low_back(matmul(low(normed), w_up) + up_bias)
    active = low(jax.nn.gelu(up_proj, approximate=False))
    lowered = low_back(matmul(active, w_down) + down_bias)
    return layer_norm(normed + lowered, ffn_gain, ffn_shift)

def reference(tokens, w_qkv, q_bias, v_bias, w_out, out_bias, attn_gain, attn_shift, w_up, up_bias, w_down, down_bias, ffn_gain, ffn_shift, seq_len, grad_pos, grad_count, out_grad):
    params = tuple((item_value.astype(jnp.float32) for item_value in (w_qkv, q_bias, v_bias, w_out, out_bias, attn_gain, attn_shift, w_up, up_bias, w_down, down_bias, ffn_gain, ffn_shift)))

    def one_sequence(running, inputs):
        seq_tokens, length, positions, pos_count, cot_values = inputs
        slot_used = (jnp.arange(PMAX) < pos_count)[:, None]
        kept_rows = jnp.where(slot_used, cot_values.astype(jnp.float32), 0.0)
        cotangent = jnp.zeros((LEN, D), jnp.float32).at[positions.astype(jnp.int32)].add(kept_rows)

        def apply_layer(params_in, tokens_in):
            return forward(params_in, tokens_in, length)
        output, pullback = jax.vjp(apply_layer, params, seq_tokens.astype(jnp.float32))
        grad_params, grad_input = pullback(cotangent)
        running = jax.tree.map(lambda first, second: first + second, running, grad_params)
        return (running, (output.astype(jnp.bfloat16), grad_input.astype(jnp.bfloat16)))
    zero_grads = jax.tree.map(jnp.zeros_like, params)
    totals, (outputs, grad_tokens) = lax.scan(one_sequence, zero_grads, (tokens, seq_len, grad_pos, grad_count, out_grad))
    return (outputs, grad_tokens, totals[0], totals[1], totals[2], totals[3], totals[4], totals[5], totals[6], totals[7], totals[8], totals[9], totals[10], totals[11], totals[12])
```

```python
import functools
import math

import jax
import jax.numpy as jnp
import numpy as np
from jax import lax
from jax.experimental import pallas as pl
from jax.experimental.pallas import tpu as pltpu
from jax.sharding import PartitionSpec as P

HEAD_DIM = 64
NORM_EPS = 1e-05
MASKED = -1000000000.0
BF = jnp.bfloat16
F32 = jnp.float32
MESH = pl.DeviceIdType.MESH
VMEM_LIMIT = 63 * 1024 * 1024


def mm(a, b):
    return lax.dot_general(a, b, (((1,), (0,)), ((), ())), preferred_element_type=F32)


def mm_nt(a, b):
    return lax.dot_general(a, b, (((1,), (1,)), ((), ())), preferred_element_type=F32)


def mm_tn(a, b):
    return lax.dot_general(a, b, (((0,), (0,)), ((), ())), preferred_element_type=F32)


def lanes(start, size):
    return pl.ds(pl.multiple_of(start, 128), size)


def gelu_cdf(u):
    return 0.5 + 0.5 * lax.erf(u * (2.0**-0.5))


def gelu_slope(u, phi):
    return phi + u * ((2.0 * math.pi) ** -0.5) * jnp.exp(-0.5 * u * u)


def norm_stats(x):
    center = x - jnp.mean(x, axis=-1, keepdims=True)
    inverse = lax.rsqrt(jnp.mean(center * center, axis=-1, keepdims=True) + NORM_EPS)
    return center * inverse, inverse


def norm_back(up, unit, inverse, gain):
    e = up * gain
    return inverse * (
        e - jnp.mean(e, axis=-1, keepdims=True) - unit * jnp.mean(e * unit, axis=-1, keepdims=True)
    )


def attend_kernel(
    tm_ref, to_ref, wm_ref, wo_ref, vec_ref, hot_ref, msk_ref,
    qkv_ref, keep_ref, send_ref, tr_ref, ctx_ref,
):
    s = lax.axis_index("seq")
    half, width = tm_ref.shape
    own = width // 2
    mine, other = lanes(s * own, own), lanes((1 - s) * own, own)
    for j in range(3):
        w_m = wm_ref[:, lanes(j * width + s * own, own)]
        w_o = wo_ref[:, j * own : (j + 1) * own]
        for b, rows in enumerate((tm_ref, to_ref)):
            acc = mm(rows[:, mine], w_m) + mm(rows[:, other], w_o)
            if j != 1:
                acc = acc + vec_ref[6 + j // 2 : 7 + j // 2, mine]
            qkv_ref[b * half : (b + 1) * half, j * own : (j + 1) * own] = acc.astype(BF)
    hot = hot_ref[...]
    tr_ref[...] = (mm(hot[:, :half], tm_ref[...]) + mm(hot[:, half:], to_ref[...])).astype(BF)
    length = 2 * half
    valid = msk_ref[...] > 0.0
    ones = jnp.ones((length, 128), BF)
    low = lax.broadcasted_iota(jnp.int32, (1, 128), 1) < HEAD_DIM
    for pair in range(own // 128):
        at = pair * 128
        keys = qkv_ref[:, own + at : own + at + 128]
        vals = jnp.concatenate([qkv_ref[:, 2 * own + at : 2 * own + at + 128], ones], axis=1)
        for b in range(2):
            q2 = qkv_ref[b * half : (b + 1) * half, at : at + 128] * jnp.array(HEAD_DIM**-0.5, BF)
            parts = []
            for e in range(2):
                q = jnp.where(low if e == 0 else ~low, q2, jnp.zeros_like(q2))
                scores = jnp.where(valid, mm_nt(q, keys), MASKED)
                top = jnp.max(scores, axis=-1, keepdims=True)
                weights = jnp.exp(scores - top).astype(BF)
                mixed = mm(weights, vals)
                parts.append(mixed[:, :128] / mixed[:, 128:])
            ctx_ref[b * half : (b + 1) * half, at : at + 128] = jnp.where(
                low, parts[0], parts[1]
            ).astype(BF)
    rows = mm(hot, ctx_ref[...]).astype(BF)
    keep_ref[:half] = ctx_ref[:half]
    send_ref[:half] = ctx_ref[half:]
    keep_ref[half:] = rows
    send_ref[half:] = rows


def feed_kernel(
    count_ref, keep_ref, recv_ref, tm_ref, tr_ref, wout_m, wout_o, wup_m, wup_o, wdn_m, wdn_o,
    vec_ref, upb_ref, grad_ref,
    out_ref, fac_ref, dat_ref, dh1_ref, dctx_ref, sums_ref,
    ab_ref, acc_ref, slope_ref, a_ref, da_ref,
):
    s = lax.axis_index("seq")
    half, width = tm_ref.shape
    own = width // 2
    total = keep_ref.shape[0]
    ff_own = wdn_m.shape[0]
    step = ff_own // 2
    mine, other = lanes(s * own, own), lanes((1 - s) * own, own)
    out_bias, gain1, shift1 = vec_ref[0:1], vec_ref[1:2], vec_ref[2:3]
    down_bias, gain2, shift2 = vec_ref[3:4], vec_ref[4:5], vec_ref[5:6]
    attn = mm(keep_ref[...], wout_m[...]) + mm(recv_ref[...], wout_o[...]) + out_bias
    tok = jnp.concatenate([tm_ref[...], tr_ref[...]], axis=0).astype(F32)
    unit1, inv1 = norm_stats(tok + attn)
    a = unit1 * gain1 + shift1
    a_ref[...] = a
    ab_ref[...] = a.astype(BF)
    unit1_r, inv1_r = unit1[half:], inv1[half:]
    acc_ref[...] = a + down_bias
    for part, (down, base) in enumerate(((wdn_m, s * ff_own), (wdn_o, (1 - s) * ff_own))):
        for c in range(ff_own // step):
            cols = lanes(base + c * step, step)
            u = mm(ab_ref[:, mine], wup_m[:, cols]) + mm(ab_ref[:, other], wup_o[:, cols])
            u = u + upb_ref[:, cols]
            phi = gelu_cdf(u)
            g = (u * phi).astype(BF)
            k = part * ff_own + c * step
            slope_ref[:, k : k + step] = gelu_slope(u[half:], phi[half:])
            acc_ref[...] += mm(g, down[c * step : (c + 1) * step])
    unit2, inv2 = norm_stats(acc_ref[...])
    out_ref[...] = (unit2[:half] * gain2 + shift2).astype(BF)
    unit2_r, inv2_r = unit2[half:], inv2[half:]
    slots = grad_ref.shape[0]
    used = lax.broadcasted_iota(jnp.int32, (slots, 1), 0) < count_ref[0]
    dy = jnp.where(used, grad_ref[...].astype(F32), 0.0)
    sums_ref[5:6] = jnp.sum(dy * unit2_r, axis=0, keepdims=True)
    sums_ref[6:7] = jnp.sum(dy, axis=0, keepdims=True)
    dh2 = norm_back(dy, unit2_r, inv2_r, gain2)
    df = dh2.astype(BF)
    for h in range(2):
        fac_ref[0, h] = ab_ref[half:, h * own : (h + 1) * own]
        fac_ref[1, h] = df[:, h * own : (h + 1) * own]
    da_m = jnp.zeros((slots, own), F32)
    da_o = jnp.zeros((slots, own), F32)
    for part, (down, base) in enumerate(((wdn_m, s * ff_own), (wdn_o, (1 - s) * ff_own))):
        for c in range(ff_own // step):
            cols = lanes(base + c * step, step)
            k = part * ff_own + c * step
            dg = mm_nt(df, down[c * step : (c + 1) * step])
            du = (dg * slope_ref[:, k : k + step]).astype(BF)
            da_m = da_m + mm_nt(du, wup_m[:, cols])
            da_o = da_o + mm_nt(du, wup_o[:, cols])
    da_ref[:, mine] = da_m
    da_ref[:, other] = da_o
    da = dh2 + da_ref[...]
    sums_ref[3:4] = jnp.sum(da * unit1_r, axis=0, keepdims=True)
    sums_ref[4:5] = jnp.sum(da, axis=0, keepdims=True)
    dh1 = norm_back(da, unit1_r, inv1_r, gain1)
    dat = dh1.astype(BF)
    sums_ref[2:3] = jnp.sum(dat.astype(F32), axis=0, keepdims=True)
    sums_ref[0:2] = jnp.zeros((2, width), F32)
    sums_ref[7:8] = jnp.zeros((1, width), F32)
    dh1_ref[...] = dh1
    dat_ref[...] = dat
    dctx_ref[...] = mm_nt(dat, wout_m[...]).astype(BF)


def back_kernel(
    qkv_ref, hot_ref, msk_ref, dctx_ref, tm_ref, to_ref, tr_ref, keep_ref, dat_ref, wm_ref, wo_ref,
    dh1_ref, sums_ref,
    load_ref, dkeep_ref, dsend_ref, small_ref,
    dp_ref, part_ref,
):
    s = lax.axis_index("seq")
    half, width = tm_ref.shape
    own = width // 2
    length = 2 * half
    slots = dctx_ref.shape[0]
    mine, other = lanes(s * own, own), lanes((1 - s) * own, own)
    scale = HEAD_DIM**-0.5
    hot = hot_ref[...]
    valid = msk_ref[...] > 0.0
    low = lax.broadcasted_iota(jnp.int32, (1, 128), 1) < HEAD_DIM
    q_rows = (mm(hot, qkv_ref[:, :own]) * scale).astype(BF)
    dq = []
    for pair in range(own // 128):
        at = pair * 128
        keys = qkv_ref[:, own + at : own + at + 128]
        vals = qkv_ref[:, 2 * own + at : 2 * own + at + 128]
        q2, c2 = q_rows[:, at : at + 128], dctx_ref[:, at : at + 128]
        zero = jnp.zeros_like(q2)
        q4 = jnp.concatenate([jnp.where(low, q2, zero), jnp.where(low, zero, q2)], axis=0)
        c4 = jnp.concatenate([jnp.where(low, c2, zero), jnp.where(low, zero, c2)], axis=0)
        scores = jnp.where(valid, mm_nt(q4, keys), MASKED)
        probs = jnp.exp(scores - jnp.max(scores, axis=-1, keepdims=True))
        probs = probs / jnp.sum(probs, axis=-1, keepdims=True)
        dprobs = mm_nt(c4, vals)
        ds = probs * (dprobs - jnp.sum(probs * dprobs, axis=-1, keepdims=True))
        ds = ds.astype(BF)
        r = mm(ds, keys) * scale
        dq.append(jnp.where(low, r[:slots], r[slots:]).astype(BF))
        dp_ref[:, own + at : own + at + 128] = mm_tn(ds, q4).astype(BF)
        dp_ref[:, 2 * own + at : 2 * own + at + 128] = mm_tn(probs.astype(BF), c4).astype(BF)
    dq = jnp.concatenate(dq, axis=1)
    dp_ref[:, :own] = mm_tn(hot, dq).astype(BF)
    for side, cols in enumerate((other, mine)):
        base = side * 3 * own
        load_ref[base : base + own] = mm_tn(tr_ref[:, cols], dq).astype(BF)
        for j in (1, 2):
            g = mm_tn(tm_ref[:, cols], dp_ref[:half, j * own : (j + 1) * own])
            g = g + mm_tn(to_ref[:, cols], dp_ref[half:, j * own : (j + 1) * own])
            load_ref[base + j * own : base + (j + 1) * own] = g.astype(BF)
    for h in range(2):
        g = mm_tn(keep_ref[half:], dat_ref[:, h * own : (h + 1) * own])
        load_ref[(6 + h) * own : (7 + h) * own] = g.astype(BF)
    if load_ref.shape[0] > 8 * own:
        load_ref[8 * own :] = jnp.zeros((load_ref.shape[0] - 8 * own, own), BF)
    p_m = jnp.zeros((length, own), F32)
    p_o = jnp.zeros((length, own), F32)
    for j in range(3):
        d = dp_ref[:, j * own : (j + 1) * own]
        p_m = p_m + mm_nt(d, wm_ref[:, lanes(j * width + s * own, own)])
        p_o = p_o + mm_nt(d, wo_ref[:, j * own : (j + 1) * own])
    part_ref[:, mine] = p_m
    part_ref[:, other] = p_o
    dh1 = dh1_ref[...]
    high = dh1.astype(BF)
    rest = (dh1 - high.astype(F32)).astype(BF)
    near = hot[:, :half]
    dkeep_ref[...] = part_ref[:half] + mm_tn(near, high) + mm_tn(near, rest)
    dsend_ref[...] = part_ref[half:].astype(BF)
    small_ref[...] = sums_ref[:, mine]
    small_ref[0:1] = jnp.sum(dq.astype(F32), axis=0, keepdims=True)
    small_ref[1:2] = jnp.sum(dp_ref[:, 2 * own :].astype(F32), axis=0, keepdims=True)


class Plan:
    def __init__(self, mesh, rows):
        axis = mesh.axis_names.index("batch")
        line = np.moveaxis(mesh.devices, axis, 0)
        line = line.reshape(line.shape[0], -1)[:, 0]
        n = len(line)
        self.n = n
        dims = []
        try:
            coords = [tuple(d.coords) for d in line]
            for d in range(3):
                size = len({c[d] for c in coords})
                if size > 1:
                    first = coords[0]
                    stride = next(
                        i
                        for i, c in enumerate(coords)
                        if c[d] != first[d] and all(c[e] == first[e] for e in range(3) if e != d)
                    )
                    dims.append((size, stride))
            good = all(
                c[d] >= 0 for c in coords for d in range(3)
            ) and math.prod(size for size, _ in dims) == n
            if not good:
                dims = []
        except (AttributeError, StopIteration):
            dims = []
        if not dims:
            rest, stride = n, 1
            while rest > 1:
                dims.append((2 if rest % 2 == 0 else rest, stride))
                stride *= dims[-1][0]
                rest //= dims[-1][0]
        dims.sort()
        self.orders = [dims]
        if len(dims) > 1:
            self.orders.append([dims[1], dims[0]] + dims[2:])
        self.peers = [(size, stride, o) for size, stride in dims for o in range(1, size)]
        unit = 16 * n
        streams = max(2, min(4, rows // unit))
        streams += streams % 2
        self.piece = -(-rows // (streams * unit)) * 16
        self.streams = streams
        self.rows = streams * n * self.piece
        self.copies = sum(size - 1 for size, _ in dims)


def coordinate(me, size, stride):
    return lax.rem(lax.div(me, stride), size)


def peer_of(me, size, stride, offset):
    here = coordinate(me, size, stride)
    there = lax.rem(here + offset, size)
    return me + (there - here) * stride, there


def reduce_kernel(
    plan, load_ref, fac_ref, small_ref,
    res_ref, got_ref, gath_ref, total_ref,
    buf_ref, in_ref, sm_ref,
    rs_send, rs_recv, ag_send, ag_recv, fa_send, fa_recv, fw_send, fw_recv, ow_send, ow_recv, sm_send, sm_recv, x_send, x_recv,
):
    me = lax.axis_index("batch")
    s = lax.axis_index("seq")
    n, piece = plan.n, plan.piece

    barrier = pltpu.get_barrier_semaphore()
    for size, stride, o in plan.peers:
        to, _ = peer_of(me, size, stride, o)
        pl.semaphore_signal(barrier, inc=1, device_id={"batch": to}, device_id_type=MESH)
    pl.semaphore_signal(barrier, inc=1, device_id={"seq": 1 - s}, device_id_type=MESH)
    pl.semaphore_wait(barrier, len(plan.peers) + 1)

    def copy(src, dst, send, recv, where):
        return pltpu.make_async_remote_copy(
            src_ref=src, dst_ref=dst, send_sem=send, recv_sem=recv, device_id=where,
            device_id_type=MESH,
        )

    def place(order):
        spots, base, span = [], jnp.int32(0), n
        for size, stride in order:
            span //= size
            spots.append((base, span))
            base = base + coordinate(me, size, stride) * span
        return spots, base

    places = [place(order) for order in plan.orders]
    pending = []

    def window(h, done, moved=None, there=None):
        spots = []
        for dim in plan.orders[0]:
            if dim == moved:
                spots.append(pl.ds(there, 1))
            elif dim in done:
                spots.append(pl.ds(0, dim[0]))
            else:
                spots.append(pl.ds(coordinate(me, *dim), 1))
        return gath_ref.at[(s, h, *spots)]

    unit = (1,) * len(plan.orders[0])
    for h in range(2):
        here = tuple(pl.ds(coordinate(me, *dim), 1) for dim in plan.orders[0])
        gath_ref[(pl.ds(s, 1), pl.ds(h, 1), *here)] = fac_ref[pl.ds(s, 1), h].reshape(
            (1, 1) + unit + fac_ref.shape[2:]
        )

    def gather_stage(level):
        started = []
        for h in range(2):
            order = plan.orders[h % len(places)]
            dim, done = order[level], order[level + 1 :]
            size, stride = dim
            here = coordinate(me, size, stride)
            for o in range(1, size):
                to, _ = peer_of(me, size, stride, o)
                sem = (h, level, o - 1)
                block = window(h, done)
                c = copy(block, block, fa_send.at[sem], fa_recv.at[sem], {"batch": to})
                c.start()
                back = lax.rem(here + size - o, size)
                started.append((c, h, level, o, window(h, done, dim, back)))
        return started

    def gather_finish(started):
        for c, h, level, o, theirs in started:
            c.wait_recv()
            sem = (h, level, o - 1)
            f = copy(
                theirs, theirs, fw_send.at[sem], fw_recv.at[sem], {"seq": 1 - s}
            )
            f.start()
            pending.append(c.wait_send)
            pending.append(f.wait)

    def reduce_start(stream, level):
        w = stream % len(places)
        order = plan.orders[w]
        base, span = places[w][0][level]
        size, stride = order[level]
        off = stream * n * piece
        ops = []
        count = sum(z - 1 for z, _ in order[:level])
        for o in range(1, size):
            to, there = peer_of(me, size, stride, o)
            src = load_ref if level == 0 else buf_ref
            at = pl.ds(pl.multiple_of(off + (base + there * span) * piece, 16), span * piece)
            slot = pl.ds(in_base(stream, level) + (o - 1) * span * piece, span * piece)
            sem = (stream, count + o - 1)
            c = copy(src.at[at], in_ref.at[slot], rs_send.at[sem], rs_recv.at[sem], {"batch": to})
            c.start()
            ops.append(c)
        return ops

    def in_base(stream, level):
        order = plan.orders[stream % len(places)]
        rows, span = 0, n
        for size, _ in order[:level]:
            span //= size
            rows += (size - 1) * span
        return (stream * n + rows) * piece

    def reduce_finish(stream, level, ops):
        w = stream % len(places)
        order = plan.orders[w]
        base, span = places[w][0][level]
        size, stride = order[level]
        off = stream * n * piece
        for c in ops:
            c.wait()
        here = coordinate(me, size, stride)
        at = pl.ds(pl.multiple_of(off + (base + here * span) * piece, 16), span * piece)
        src = load_ref if level == 0 else buf_ref
        acc = src[at].astype(F32)
        for o in range(1, size):
            slot = pl.ds(in_base(stream, level) + (o - 1) * span * piece, span * piece)
            acc = acc + in_ref[slot].astype(F32)
        dst = res_ref if level == len(order) - 1 else buf_ref
        dst[at] = acc.astype(BF)

    def spread_start(stream, level):
        w = stream % len(places)
        order = plan.orders[w]
        base, span = places[w][0][level]
        size, stride = order[level]
        off = stream * n * piece
        here = coordinate(me, size, stride)
        at = pl.ds(pl.multiple_of(off + (base + here * span) * piece, 16), span * piece)
        count = sum(z - 1 for z, _ in order[:level])
        ops = []
        for o in range(1, size):
            to, _ = peer_of(me, size, stride, o)
            sem = (stream, count + o - 1)
            c = copy(res_ref.at[at], res_ref.at[at], ag_send.at[sem], ag_recv.at[sem], {"batch": to})
            c.start()
            ops.append(c)
        return ops

    def small_start(level, value):
        size, stride = plan.orders[0][level]
        here = coordinate(me, size, stride)
        first = sum(z for z, _ in plan.orders[0][:level])
        sm_ref[pl.ds(first + here, 1)] = value[None]
        ops = []
        for o in range(1, size):
            to, _ = peer_of(me, size, stride, o)
            sem = first + o
            slot = pl.ds(first + here, 1)
            c = copy(sm_ref.at[slot], sm_ref.at[slot], sm_send.at[sem], sm_recv.at[sem], {"batch": to})
            c.start()
            ops.append(c)
        return ops

    def small_finish(level, ops):
        for c in ops:
            c.wait()
        size, _ = plan.orders[0][level]
        first = sum(z for z, _ in plan.orders[0][:level])
        acc = sm_ref[first]
        for o in range(1, size):
            acc = acc + sm_ref[first + o]
        return acc

    levels = len(plan.orders[0])
    last = levels - 1
    running = {t: reduce_start(t, 0) for t in range(plan.streams)}
    gathers = gather_stage(last)
    for h in range(2):
        own_copy = copy(
            window(h, ()), window(h, ()), ow_send.at[h], ow_recv.at[h], {"seq": 1 - s}
        )
        own_copy.start()
        pending.append(own_copy.wait)
    small = small_ref[...]
    for level in range(levels):
        small_ops = small_start(level, small)
        gather_finish(gathers)
        gathers = gather_stage(last - 1 - level) if level < last else []
        for t in range(plan.streams):
            reduce_finish(t, level, running[t])
            running[t] = reduce_start(t, level + 1) if level < last else spread_start(t, last)
        small = small_finish(level, small_ops)
    total_ref[...] = small
    cross = got_ref.shape[0]
    span = n * piece
    for level in range(last, -1, -1):
        for t in range(plan.streams):
            for c in running[t]:
                c.wait()
            if level > 0:
                running[t] = spread_start(t, level - 1)
            elif t * span < cross:
                rows = pl.ds(t * span, min(span, cross - t * span))
                x = copy(res_ref.at[rows], got_ref.at[rows], x_send.at[t], x_recv.at[t], {"seq": 1 - s})
                x.start()
                pending.append(x.wait)
    for wait in pending:
        wait()


def ffn_kernel(
    gath_ref, wup_m, wup_o, wdn_m, upb_ref,
    gdn_ref, gup_ref, gsend_ref, bias_ref, dbias_ref,
    far_ref,
):
    s = lax.axis_index("seq")
    step, steps = pl.program_id(0), pl.num_programs(0)
    own = gath_ref.shape[3]
    ff_own = wdn_m.shape[0]
    size = 512 if ff_own % 512 == 0 else ff_own
    sides = pl.ds(s, 1), pl.ds(1 - s, 1)

    @pl.when(step == 0)
    def _():
        for ref in (gdn_ref, gup_ref, far_ref, bias_ref, dbias_ref):
            ref[...] = jnp.zeros_like(ref)

    for h in range(2):
        dbias_ref[h : h + 1] += jnp.sum(gath_ref[1, h].astype(F32), axis=0, keepdims=True)
    for c in range(ff_own // size):
        cols = lanes(s * ff_own + c * size, size)
        at = slice(c * size, (c + 1) * size)
        u = mm(gath_ref[0, sides[0]][0], wup_m[:, cols])
        u = u + mm(gath_ref[0, sides[1]][0], wup_o[:, cols]) + upb_ref[:, cols]
        phi = gelu_cdf(u)
        g = (u * phi).astype(BF)
        dg = mm_nt(gath_ref[1, 0], wdn_m[at, :own]) + mm_nt(gath_ref[1, 1], wdn_m[at, own:])
        du = (dg * gelu_slope(u, phi)).astype(BF)
        bias_ref[:, at] += jnp.sum(du.astype(F32), axis=0, keepdims=True)
        for h in range(2):
            gdn_ref[at, h * own : (h + 1) * own] += mm_tn(g, gath_ref[1, h])
        gup_ref[:, at] += mm_tn(gath_ref[0, sides[0]][0], du)
        far_ref[:, at] += mm_tn(gath_ref[0, sides[1]][0], du)

    @pl.when(step == steps - 1)
    def _():
        gsend_ref[...] = far_ref[...].astype(BF)


def final_kernel(res_ref, got_ref, gup_ref, grecv_ref, gqkv_out, gout_out, gup_out):
    s = lax.axis_index("seq")
    own = gout_out.shape[0]
    width, ff_own = 2 * own, gup_ref.shape[1]
    for j in range(3):
        gqkv_out[:, lanes(j * width + s * own, own)] = res_ref[(3 + j) * own : (4 + j) * own].astype(F32)
        gqkv_out[:, lanes(j * width + (1 - s) * own, own)] = got_ref[j * own : (j + 1) * own].astype(F32)
    for h in range(2):
        gout_out[:, h * own : (h + 1) * own] = res_ref[(6 + h) * own : (7 + h) * own].astype(F32)
    gup_out[:, lanes(s * ff_own, ff_own)] = gup_ref[...]
    gup_out[:, lanes((1 - s) * ff_own, ff_own)] = grecv_ref[...].astype(F32)


def shape(dims, kind=BF):
    return jax.ShapeDtypeStruct(dims, kind)


def local_call(kernel, outs, scratch=(), scalars=0, args=0):
    extra = {}
    if scalars:
        extra["in_specs"] = [pl.BlockSpec(memory_space=pltpu.SMEM)] * scalars + [
            pl.BlockSpec(memory_space=pltpu.VMEM)
        ] * (args - scalars)
    return pl.pallas_call(
        kernel,
        out_shape=outs,
        scratch_shapes=scratch,
        compiler_params=pltpu.CompilerParams(vmem_limit_bytes=VMEM_LIMIT),
        **extra,
    )


def body(
    mesh, tokens, w_qkv, q_bias, v_bias, w_out, out_bias, attn_gain, attn_shift, w_up, up_bias,
    w_down, down_bias, ffn_gain, ffn_shift, seq_len, grad_pos, grad_count, out_grad,
):
    half, width = tokens.shape[1:]
    own, ff_own = w_qkv.shape[0], w_down.shape[0]
    length, slots, ff = 2 * half, grad_pos.shape[1], 2 * ff_own
    plan = Plan(mesh, 8 * own)
    n = plan.n
    s = lax.axis_index("seq")
    swap = lambda x: lax.ppermute(x, "seq", [(0, 1), (1, 0)])
    tm = tokens[0]
    cols = jnp.concatenate(
        [lax.dynamic_slice_in_dim(w_qkv, j * width + (1 - s) * own, own, 1) for j in range(3)], axis=1
    )
    to, wqkv_o = swap(tm), swap(cols)
    wout_o, wup_o, wdn_o = swap(w_out), swap(w_up), swap(w_down)
    vec = jnp.stack(
        [out_bias, attn_gain, attn_shift, down_bias, ffn_gain, ffn_shift, q_bias, v_bias]
    )
    upb = up_bias.reshape(1, ff)
    row = jnp.arange(length, dtype=jnp.int32)
    pos = jnp.where(row < half, row + s * half, row - half + (1 - s) * half)
    live = jnp.arange(slots)[:, None] < grad_count[0]
    hot = ((grad_pos[0][:, None] == pos[None, :]) & live).astype(BF)
    msk = (pos < seq_len[0]).astype(F32)[None]

    qkv, keep, send, tr = local_call(
        attend_kernel,
        [shape((length, 3 * own)), shape((half + slots, own)), shape((half + slots, own)),
         shape((slots, width))],
        [pltpu.VMEM((length, own), BF)],
    )(tm, to, w_qkv, wqkv_o, vec, hot, msk)
    recv = swap(send)
    out, fac, dat, dh1, dctx, sums = local_call(
        feed_kernel,
        [shape((half, width)), shape((2, 2, slots, own)), shape((slots, width)),
         shape((slots, width), F32), shape((slots, own)), shape((8, width), F32)],
        [pltpu.VMEM((half + slots, width), BF), pltpu.VMEM((half + slots, width), F32),
         pltpu.VMEM((slots, ff), F32), pltpu.VMEM((half + slots, width), F32),
         pltpu.VMEM((slots, width), F32)],
        scalars=1, args=14,
    )(grad_count, keep, recv, tm, tr, w_out, wout_o, w_up, wup_o, w_down, wdn_o, vec, upb, out_grad[0])
    load, dkeep, dsend, small = local_call(
        back_kernel,
        [shape((plan.rows, own)), shape((half, width), F32), shape((half, width)),
         shape((8, own), F32)],
        [pltpu.VMEM((length, 3 * own), BF), pltpu.VMEM((length, width), F32)],
    )(qkv, hot, msk, dctx, tm, to, tr, keep, dat, w_qkv, wqkv_o, dh1, sums)
    drecv = swap(dsend)
    grad_tok = (dkeep + drecv.astype(F32)).astype(BF)[None]

    dma = pltpu.SemaphoreType.DMA
    depth, widest = len(plan.orders[0]), max(size for size, _ in plan.orders[0]) - 1
    slots_small = sum(size for size, _ in plan.orders[0])
    cross = 3 * own
    res, got, gath, total = pl.pallas_call(
        functools.partial(reduce_kernel, plan),
        out_shape=[shape((plan.rows, own)), shape((cross, own)), shape((2, 2, *(size for size, _ in plan.orders[0]), slots, own)),
                   shape((8, own), F32)],
        scratch_shapes=[
            pltpu.VMEM((plan.rows, own), BF), pltpu.VMEM((plan.rows, own), BF),
            pltpu.VMEM((slots_small, 8, own), F32),
            dma((plan.streams, plan.copies)), dma((plan.streams, plan.copies)),
            dma((plan.streams, plan.copies)), dma((plan.streams, plan.copies)),
            dma((2, depth, widest)), dma((2, depth, widest)),
            dma((2, depth, widest)), dma((2, depth, widest)),
            dma((2,)), dma((2,)),
            dma((slots_small,)), dma((slots_small,)),
            dma((plan.streams,)), dma((plan.streams,)),
        ],
        compiler_params=pltpu.CompilerParams(
            collective_id=0, has_side_effects=True, vmem_limit_bytes=VMEM_LIMIT
        ),
    )(load, fac, small)

    rows = n * slots
    tile = rows if rows <= 1280 else 1280 if rows % 1280 == 0 else slots
    fixed = lambda *dims: pl.BlockSpec(dims, lambda i: (0,) * len(dims), pipeline_mode=pl.Buffered(1))
    gdn, gup, gsend, ubias, dbias = pl.pallas_call(
        ffn_kernel,
        grid=(rows // tile,),
        in_specs=[pl.BlockSpec((2, 2, tile, own), lambda i: (0, 0, i, 0)), fixed(own, ff),
                  fixed(own, ff), fixed(ff_own, width), fixed(1, ff)],
        out_specs=[fixed(ff_own, width), fixed(own, ff_own), fixed(own, ff_own), fixed(1, ff_own),
                   fixed(2, own)],
        out_shape=[shape((ff_own, width), F32), shape((own, ff_own), F32), shape((own, ff_own)),
                   shape((1, ff_own), F32), shape((2, own), F32)],
        scratch_shapes=[pltpu.VMEM((own, ff_own), F32)],
        compiler_params=pltpu.CompilerParams(vmem_limit_bytes=VMEM_LIMIT),
    )(gath.reshape(2, 2, rows, own), w_up, wup_o, w_down, upb)
    grecv = swap(gsend)
    gqkv, gout, gup = local_call(
        final_kernel,
        [shape((own, 3 * width), F32), shape((own, width), F32), shape((own, ff), F32)],
    )(res, got, gup, grecv)
    return (
        out[None], grad_tok, gqkv, total[0], total[1], gout, total[2], total[3], total[4], gup,
        ubias[0], gdn, lax.dynamic_index_in_dim(dbias, s, 0, keepdims=False), total[5], total[6],
    )


def solution(mesh):
    specs = dict(
        in_specs=(
            P("batch", "seq", None), P("seq", None), P(), P(), P("seq", None), P(), P(), P(),
            P("seq", None), P(), P("seq", None), P(), P(), P(), P("batch"), P("batch", None),
            P("batch"), P("batch", None, None),
        ),
        out_specs=(
            P("batch", "seq", None), P("batch", "seq", None), P("seq", None), P("seq"), P("seq"),
            P("seq", None), P("seq"), P("seq"), P("seq"), P("seq", None), P("seq"),
            P("seq", None), P("seq"), P("seq"), P("seq"),
        ),
    )
    return jax.shard_map(functools.partial(body, mesh), mesh=mesh, check_vma=False, **specs)
```

```python
import functools
import math

import jax
import jax.numpy as jnp
import numpy as np
from jax import lax
from jax.experimental import pallas as pl
from jax.experimental.pallas import tpu as pltpu
from jax.sharding import PartitionSpec as P

HEAD_DIM = 64
NORM_EPS = 1e-05
MASKED = -1000000000.0
BF = jnp.bfloat16
F32 = jnp.float32
MESH = pl.DeviceIdType.MESH
VMEM_LIMIT = 63 * 1024 * 1024


def mm(a, b):
    return lax.dot_general(a, b, (((1,), (0,)), ((), ())), preferred_element_type=F32)


def mm_nt(a, b):
    return lax.dot_general(a, b, (((1,), (1,)), ((), ())), preferred_element_type=F32)


def mm_tn(a, b):
    return lax.dot_general(a, b, (((0,), (0,)), ((), ())), preferred_element_type=F32)


def lanes(start, size):
    return pl.ds(pl.multiple_of(start, 128), size)


def gelu_cdf(u):
    return 0.5 + 0.5 * lax.erf(u * (2.0**-0.5))


def gelu_slope(u, phi):
    return phi + u * ((2.0 * math.pi) ** -0.5) * jnp.exp(-0.5 * u * u)


def norm_stats(x):
    center = x - jnp.mean(x, axis=-1, keepdims=True)
    inverse = lax.rsqrt(jnp.mean(center * center, axis=-1, keepdims=True) + NORM_EPS)
    return center * inverse, inverse


def norm_back(up, unit, inverse, gain):
    e = up * gain
    return inverse * (
        e - jnp.mean(e, axis=-1, keepdims=True) - unit * jnp.mean(e * unit, axis=-1, keepdims=True)
    )


def attend_kernel(
    tm_ref, to_ref, wm_ref, wo_ref, vec_ref, hot_ref, msk_ref,
    qkv_ref, keep_ref, send_ref, tr_ref, crow_ref, ctx_ref,
):
    s = lax.axis_index("seq")
    half, width = tm_ref.shape
    own = width // 2
    mine, other = lanes(s * own, own), lanes((1 - s) * own, own)
    for j in range(3):
        w_m = wm_ref[:, lanes(j * width + s * own, own)]
        w_o = wo_ref[:, j * own : (j + 1) * own]
        for b, rows in enumerate((tm_ref, to_ref)):
            acc = mm(rows[:, mine], w_m) + mm(rows[:, other], w_o)
            if j != 1:
                acc = acc + vec_ref[6 + j // 2 : 7 + j // 2, mine]
            qkv_ref[b * half : (b + 1) * half, j * own : (j + 1) * own] = acc.astype(BF)
    hot = hot_ref[...]
    tr_ref[...] = (mm(hot[:, :half], tm_ref[...]) + mm(hot[:, half:], to_ref[...])).astype(BF)
    length = 2 * half
    valid = msk_ref[...] > 0.0
    ones = jnp.ones((length, 128), BF)
    low = lax.broadcasted_iota(jnp.int32, (1, 128), 1) < HEAD_DIM
    for pair in range(own // 128):
        at = pair * 128
        keys = qkv_ref[:, own + at : own + at + 128]
        vals = jnp.concatenate([qkv_ref[:, 2 * own + at : 2 * own + at + 128], ones], axis=1)
        for b in range(2):
            q2 = qkv_ref[b * half : (b + 1) * half, at : at + 128] * jnp.array(HEAD_DIM**-0.5, BF)
            parts = []
            for e in range(2):
                q = jnp.where(low if e == 0 else ~low, q2, jnp.zeros_like(q2))
                scores = jnp.where(valid, mm_nt(q, keys), MASKED)
                top = jnp.max(scores, axis=-1, keepdims=True)
                weights = jnp.exp(scores - top).astype(BF)
                mixed = mm(weights, vals)
                parts.append(mixed[:, :128] / mixed[:, 128:])
            ctx_ref[b * half : (b + 1) * half, at : at + 128] = jnp.where(
                low, parts[0], parts[1]
            ).astype(BF)
    rows = mm(hot, ctx_ref[...]).astype(BF)
    keep_ref[:half] = ctx_ref[:half]
    send_ref[:half] = ctx_ref[half:]
    keep_ref[half:] = rows
    crow_ref[...] = rows
    send_ref[half:] = rows


def feed_kernel(
    count_ref, keep_ref, recv_ref, tm_ref, tr_ref, wout_m, wout_o, wup_m, wup_o, wdn_m, wdn_o,
    vec_ref, upb_ref, grad_ref,
    out_ref, fac_ref, dat_ref, dh1_ref, dctx_ref, sums_ref,
    ab_ref, acc_ref, slope_ref, a_ref, da_ref,
):
    s = lax.axis_index("seq")
    half, width = tm_ref.shape
    own = width // 2
    total = keep_ref.shape[0]
    ff_own = wdn_m.shape[0]
    step = ff_own // 2
    mine, other = lanes(s * own, own), lanes((1 - s) * own, own)
    out_bias, gain1, shift1 = vec_ref[0:1], vec_ref[1:2], vec_ref[2:3]
    down_bias, gain2, shift2 = vec_ref[3:4], vec_ref[4:5], vec_ref[5:6]
    attn = mm(keep_ref[...], wout_m[...]) + mm(recv_ref[...], wout_o[...]) + out_bias
    tok = jnp.concatenate([tm_ref[...], tr_ref[...]], axis=0).astype(F32)
    unit1, inv1 = norm_stats(tok + attn)
    a = unit1 * gain1 + shift1
    a_ref[...] = a
    ab_ref[...] = a.astype(BF)
    unit1_r, inv1_r = unit1[half:], inv1[half:]
    acc_ref[...] = a + down_bias
    for part, (down, base) in enumerate(((wdn_m, s * ff_own), (wdn_o, (1 - s) * ff_own))):
        for c in range(ff_own // step):
            cols = lanes(base + c * step, step)
            u = mm(ab_ref[:, mine], wup_m[:, cols]) + mm(ab_ref[:, other], wup_o[:, cols])
            u = u + upb_ref[:, cols]
            phi = gelu_cdf(u)
            g = (u * phi).astype(BF)
            k = part * ff_own + c * step
            slope_ref[:, k : k + step] = gelu_slope(u[half:], phi[half:])
            acc_ref[...] += mm(g, down[c * step : (c + 1) * step])
    unit2, inv2 = norm_stats(acc_ref[...])
    out_ref[...] = (unit2[:half] * gain2 + shift2).astype(BF)
    unit2_r, inv2_r = unit2[half:], inv2[half:]
    slots = grad_ref.shape[0]
    used = lax.broadcasted_iota(jnp.int32, (slots, 1), 0) < count_ref[0]
    dy = jnp.where(used, grad_ref[...].astype(F32), 0.0)
    sums_ref[5:6] = jnp.sum(dy * unit2_r, axis=0, keepdims=True)
    sums_ref[6:7] = jnp.sum(dy, axis=0, keepdims=True)
    dh2 = norm_back(dy, unit2_r, inv2_r, gain2)
    df = dh2.astype(BF)
    for h in range(2):
        fac_ref[0, h] = ab_ref[half:, h * own : (h + 1) * own]
        fac_ref[1, h] = df[:, h * own : (h + 1) * own]
    da_m = jnp.zeros((slots, own), F32)
    da_o = jnp.zeros((slots, own), F32)
    for part, (down, base) in enumerate(((wdn_m, s * ff_own), (wdn_o, (1 - s) * ff_own))):
        for c in range(ff_own // step):
            cols = lanes(base + c * step, step)
            k = part * ff_own + c * step
            dg = mm_nt(df, down[c * step : (c + 1) * step])
            du = (dg * slope_ref[:, k : k + step]).astype(BF)
            da_m = da_m + mm_nt(du, wup_m[:, cols])
            da_o = da_o + mm_nt(du, wup_o[:, cols])
    da_ref[:, mine] = da_m
    da_ref[:, other] = da_o
    da = dh2 + da_ref[...]
    sums_ref[3:4] = jnp.sum(da * unit1_r, axis=0, keepdims=True)
    sums_ref[4:5] = jnp.sum(da, axis=0, keepdims=True)
    dh1 = norm_back(da, unit1_r, inv1_r, gain1)
    dat = dh1.astype(BF)
    sums_ref[2:3] = jnp.sum(dat.astype(F32), axis=0, keepdims=True)
    sums_ref[0:2] = jnp.zeros((2, width), F32)
    sums_ref[7:8] = jnp.zeros((1, width), F32)
    dh1_ref[...] = dh1
    dat_ref[...] = dat
    dctx_ref[...] = mm_nt(dat, wout_m[...]).astype(BF)


class Plan:
    def __init__(self, mesh, rows):
        axis = mesh.axis_names.index("batch")
        line = np.moveaxis(mesh.devices, axis, 0)
        line = line.reshape(line.shape[0], -1)[:, 0]
        n = len(line)
        self.n = n
        dims = []
        try:
            coords = [tuple(d.coords) for d in line]
            for d in range(3):
                size = len({c[d] for c in coords})
                if size > 1:
                    first = coords[0]
                    stride = next(
                        i
                        for i, c in enumerate(coords)
                        if c[d] != first[d] and all(c[e] == first[e] for e in range(3) if e != d)
                    )
                    dims.append((size, stride))
            good = all(
                c[d] >= 0 for c in coords for d in range(3)
            ) and math.prod(size for size, _ in dims) == n
            if not good:
                dims = []
        except (AttributeError, StopIteration):
            dims = []
        if not dims:
            rest, stride = n, 1
            while rest > 1:
                dims.append((2 if rest % 2 == 0 else rest, stride))
                stride *= dims[-1][0]
                rest //= dims[-1][0]
        dims.sort()
        self.orders = [dims]
        if len(dims) > 1:
            self.orders.append([dims[1], dims[0]] + dims[2:])
        self.peers = [(size, stride, o) for size, stride in dims for o in range(1, size)]
        unit = 16 * n
        streams = max(2, min(4, rows // unit))
        streams += streams % 2
        self.piece = -(-rows // (streams * unit)) * 16
        self.streams = streams
        self.rows = streams * n * self.piece
        self.copies = sum(size - 1 for size, _ in dims)


def coordinate(me, size, stride):
    return lax.rem(lax.div(me, stride), size)


def peer_of(me, size, stride, offset):
    here = coordinate(me, size, stride)
    there = lax.rem(here + offset, size)
    return me + (there - here) * stride, there


def reduce_kernel(
    plan, fused,
    fac_ref, qkv_ref, hot_ref, msk_ref, dctx_ref, tm_ref, to_ref, tr_ref, crow_ref, dat_ref, dh1_ref,
    sums_ref, wqm_any, wqo_any, wum_any, wuo_any, wdm_any, upb_ref,
    res_ref, got_ref, gath_ref, total_ref, dkeep_ref, drecv_ref, gdn_ref, gup_ref, gfar_ref, ubias_ref,
    dbias_ref,
    load_ref, buf_ref, in_ref, sm_ref, dp_ref, part_ref, dsend_ref, gnear_ref,
    wqm_ref, wqo_ref, wum_ref, wuo_ref, wdm_ref,
    rs_send, rs_recv, ag_send, ag_recv, fa_send, fa_recv, fw_send, fw_recv, ow_send, ow_recv,
    sm_send, sm_recv, x_send, x_recv, d_send, d_recv, u_send, u_recv, w_sem,
):
    me = lax.axis_index("batch")
    s = lax.axis_index("seq")
    n, piece = plan.n, plan.piece
    half, width = tm_ref.shape
    own = width // 2
    length = 2 * half
    slots = dctx_ref.shape[0]
    mine, other = lanes(s * own, own), lanes((1 - s) * own, own)
    partner = {"seq": 1 - s}

    fetched = [(wqm_any, wqm_ref), (wqo_any, wqo_ref)]
    if fused:
        fetched += [(wum_any, wum_ref), (wuo_any, wuo_ref), (wdm_any, wdm_ref)]
    fetches = [pltpu.make_async_copy(a, b, w_sem.at[i]) for i, (a, b) in enumerate(fetched)]
    for f in fetches:
        f.start()

    barrier = pltpu.get_barrier_semaphore()
    for size, stride, o in plan.peers:
        to, _ = peer_of(me, size, stride, o)
        pl.semaphore_signal(barrier, inc=1, device_id={"batch": to}, device_id_type=MESH)
    pl.semaphore_signal(barrier, inc=1, device_id=partner, device_id_type=MESH)
    pl.semaphore_wait(barrier, len(plan.peers) + 1)

    def copy(src, dst, send, recv, where):
        return pltpu.make_async_remote_copy(
            src_ref=src, dst_ref=dst, send_sem=send, recv_sem=recv, device_id=where,
            device_id_type=MESH,
        )

    def place(order):
        spots, base, span = [], jnp.int32(0), n
        for size, stride in order:
            span //= size
            spots.append((base, span))
            base = base + coordinate(me, size, stride) * span
        return spots, base

    places = [place(order) for order in plan.orders]
    pending = []

    def window(h, done, moved=None, there=None):
        spots = []
        for dim in plan.orders[0]:
            if dim == moved:
                spots.append(pl.ds(there, 1))
            elif dim in done:
                spots.append(pl.ds(0, dim[0]))
            else:
                spots.append(pl.ds(coordinate(me, *dim), 1))
        return gath_ref.at[(s, h, *spots)]

    unit = (1,) * len(plan.orders[0])
    for h in range(2):
        here = tuple(pl.ds(coordinate(me, *dim), 1) for dim in plan.orders[0])
        gath_ref[(pl.ds(s, 1), pl.ds(h, 1), *here)] = fac_ref[pl.ds(s, 1), h].reshape(
            (1, 1) + unit + fac_ref.shape[2:]
        )

    def gather_stage(level):
        started = []
        for h in range(2):
            order = plan.orders[h % len(places)]
            dim, done = order[level], order[level + 1 :]
            size, stride = dim
            here = coordinate(me, size, stride)
            for o in range(1, size):
                to, _ = peer_of(me, size, stride, o)
                sem = (h, level, o - 1)
                block = window(h, done)
                c = copy(block, block, fa_send.at[sem], fa_recv.at[sem], {"batch": to})
                c.start()
                back = lax.rem(here + size - o, size)
                started.append((c, h, level, o, window(h, done, dim, back)))
        return started

    def gather_finish(started):
        for c, h, level, o, theirs in started:
            c.wait_recv()
            sem = (h, level, o - 1)
            f = copy(
                theirs, theirs, fw_send.at[sem], fw_recv.at[sem], {"seq": 1 - s}
            )
            f.start()
            pending.append(c.wait_send)
            pending.append(f.wait)

    def reduce_start(stream, level):
        w = stream % len(places)
        order = plan.orders[w]
        base, span = places[w][0][level]
        size, stride = order[level]
        off = stream * n * piece
        ops = []
        count = sum(z - 1 for z, _ in order[:level])
        for o in range(1, size):
            to, there = peer_of(me, size, stride, o)
            src = load_ref if level == 0 else buf_ref
            at = pl.ds(pl.multiple_of(off + (base + there * span) * piece, 16), span * piece)
            slot = pl.ds(in_base(stream, level) + (o - 1) * span * piece, span * piece)
            sem = (stream, count + o - 1)
            c = copy(src.at[at], in_ref.at[slot], rs_send.at[sem], rs_recv.at[sem], {"batch": to})
            c.start()
            ops.append(c)
        return ops

    def in_base(stream, level):
        order = plan.orders[stream % len(places)]
        rows, span = 0, n
        for size, _ in order[:level]:
            span //= size
            rows += (size - 1) * span
        return (stream * n + rows) * piece

    def reduce_finish(stream, level, ops):
        w = stream % len(places)
        order = plan.orders[w]
        base, span = places[w][0][level]
        size, stride = order[level]
        off = stream * n * piece
        for c in ops:
            c.wait()
        here = coordinate(me, size, stride)
        at = pl.ds(pl.multiple_of(off + (base + here * span) * piece, 16), span * piece)
        src = load_ref if level == 0 else buf_ref
        acc = src[at].astype(F32)
        for o in range(1, size):
            slot = pl.ds(in_base(stream, level) + (o - 1) * span * piece, span * piece)
            acc = acc + in_ref[slot].astype(F32)
        dst = res_ref if level == len(order) - 1 else buf_ref
        dst[at] = acc.astype(BF)

    def spread_start(stream, level):
        w = stream % len(places)
        order = plan.orders[w]
        base, span = places[w][0][level]
        size, stride = order[level]
        off = stream * n * piece
        here = coordinate(me, size, stride)
        at = pl.ds(pl.multiple_of(off + (base + here * span) * piece, 16), span * piece)
        count = sum(z - 1 for z, _ in order[:level])
        ops = []
        for o in range(1, size):
            to, _ = peer_of(me, size, stride, o)
            sem = (stream, count + o - 1)
            c = copy(res_ref.at[at], res_ref.at[at], ag_send.at[sem], ag_recv.at[sem], {"batch": to})
            c.start()
            ops.append(c)
        return ops

    def small_start(level, value):
        size, stride = plan.orders[0][level]
        here = coordinate(me, size, stride)
        first = sum(z for z, _ in plan.orders[0][:level])
        sm_ref[pl.ds(first + here, 1)] = value[None]
        ops = []
        for o in range(1, size):
            to, _ = peer_of(me, size, stride, o)
            sem = first + o
            slot = pl.ds(first + here, 1)
            c = copy(sm_ref.at[slot], sm_ref.at[slot], sm_send.at[sem], sm_recv.at[sem], {"batch": to})
            c.start()
            ops.append(c)
        return ops

    def small_finish(level, ops):
        for c in ops:
            c.wait()
        size, _ = plan.orders[0][level]
        first = sum(z for z, _ in plan.orders[0][:level])
        acc = sm_ref[first]
        for o in range(1, size):
            acc = acc + sm_ref[first + o]
        return acc

    levels = len(plan.orders[0])
    last = levels - 1
    span = n * piece
    gathers = gather_stage(last)
    for h in range(2):
        c = copy(window(h, ()), window(h, ()), ow_send.at[h], ow_recv.at[h], partner)
        c.start()
        pending.append(c.wait)

    running = {}
    ready = set()

    def finished(first, end):
        ready.update(range(first, end))
        for t in range(plan.streams):
            rows = [r for r in range(t * span, (t + 1) * span, own) if r < 8 * own]
            if t not in running and all(r // own in ready for r in rows) and (
                (min((t + 1) * span, 8 * own) - 1) // own in ready
            ):
                running[t] = reduce_start(t, 0)

    if load_ref.shape[0] > 8 * own:
        load_ref[8 * own :] = jnp.zeros((load_ref.shape[0] - 8 * own, own), BF)
    for h in range(2):
        g = mm_tn(crow_ref[...], dat_ref[:, h * own : (h + 1) * own])
        load_ref[(6 + h) * own : (7 + h) * own] = g.astype(BF)
    finished(6, 8)

    scale = HEAD_DIM**-0.5
    hot = hot_ref[...]
    valid = msk_ref[...] > 0.0
    low = lax.broadcasted_iota(jnp.int32, (1, 128), 1) < HEAD_DIM
    q_rows = (mm(hot, qkv_ref[:, :own]) * scale).astype(BF)
    dq = []
    for pair in range(own // 128):
        at = pair * 128
        keys = qkv_ref[:, own + at : own + at + 128]
        vals = qkv_ref[:, 2 * own + at : 2 * own + at + 128]
        q2, c2 = q_rows[:, at : at + 128], dctx_ref[:, at : at + 128]
        zero = jnp.zeros_like(q2)
        q4 = jnp.concatenate([jnp.where(low, q2, zero), jnp.where(low, zero, q2)], axis=0)
        c4 = jnp.concatenate([jnp.where(low, c2, zero), jnp.where(low, zero, c2)], axis=0)
        scores = jnp.where(valid, mm_nt(q4, keys), MASKED)
        probs = jnp.exp(scores - jnp.max(scores, axis=-1, keepdims=True))
        probs = probs / jnp.sum(probs, axis=-1, keepdims=True)
        dprobs = mm_nt(c4, vals)
        ds = probs * (dprobs - jnp.sum(probs * dprobs, axis=-1, keepdims=True))
        ds = ds.astype(BF)
        r = mm(ds, keys) * scale
        dq.append(jnp.where(low, r[:slots], r[slots:]).astype(BF))
        dp_ref[:, own + at : own + at + 128] = mm_tn(ds, q4).astype(BF)
        dp_ref[:, 2 * own + at : 2 * own + at + 128] = mm_tn(probs.astype(BF), c4).astype(BF)
    dq = jnp.concatenate(dq, axis=1)
    for side, cols in enumerate((other, mine)):
        for j in range(3):
            if j == 0:
                g = mm_tn(tr_ref[:, cols], dq)
            else:
                g = mm_tn(tm_ref[:, cols], dp_ref[:half, j * own : (j + 1) * own])
                g = g + mm_tn(to_ref[:, cols], dp_ref[half:, j * own : (j + 1) * own])
            section = side * 3 + j
            load_ref[section * own : (section + 1) * own] = g.astype(BF)
            finished(section, section + 1)

    dp_ref[:, :own] = mm_tn(hot, dq).astype(BF)
    for f in fetches[:2]:
        f.wait()
    p_m = jnp.zeros((length, own), F32)
    p_o = jnp.zeros((length, own), F32)
    for j in range(3):
        d = dp_ref[:, j * own : (j + 1) * own]
        p_m = p_m + mm_nt(d, wqm_ref[:, lanes(j * width + s * own, own)])
        p_o = p_o + mm_nt(d, wqo_ref[:, j * own : (j + 1) * own])
    part_ref[:, mine] = p_m
    part_ref[:, other] = p_o
    dsend_ref[...] = part_ref[half:].astype(BF)
    c = copy(dsend_ref, drecv_ref, d_send, d_recv, partner)
    c.start()
    pending.append(c.wait)
    dh1 = dh1_ref[...]
    high = dh1.astype(BF)
    rest = (dh1 - high.astype(F32)).astype(BF)
    near = hot[:, :half]
    dkeep_ref[...] = part_ref[:half] + mm_tn(near, high) + mm_tn(near, rest)
    small = sums_ref[:, mine]
    row = lax.broadcasted_iota(jnp.int32, (8, 1), 0)
    q_sum = jnp.sum(dq.astype(F32), axis=0, keepdims=True)
    v_sum = jnp.sum(dp_ref[:, 2 * own :].astype(F32), axis=0, keepdims=True)
    small = jnp.where(row == 0, q_sum, jnp.where(row == 1, v_sum, small))
    gather_finish(gathers)
    gathers = gather_stage(last - 1) if last >= 1 else []

    chunks = []
    if fused:
        ff_own = wdm_ref.shape[0]
        size = 256 if ff_own % 256 == 0 else ff_own
        rows = n * slots

        def factor(kind, h):
            value = gath_ref[kind, h] if isinstance(h, int) else gath_ref[kind, pl.ds(h, 1)]
            return value.reshape(rows, own)

        def chunk(c):
            cols = lanes(s * ff_own + c * size, size)
            at = slice(c * size, (c + 1) * size)
            near_x, far_x = factor(0, s), factor(0, 1 - s)
            u = mm(near_x, wum_ref[:, cols]) + mm(far_x, wuo_ref[:, cols]) + upb_ref[:, cols]
            phi = gelu_cdf(u)
            g = (u * phi).astype(BF)
            dg = mm_nt(factor(1, 0), wdm_ref[at, :own]) + mm_nt(factor(1, 1), wdm_ref[at, own:])
            du = (dg * gelu_slope(u, phi)).astype(BF)
            ubias_ref[:, at] = jnp.sum(du.astype(F32), axis=0, keepdims=True)
            for h in range(2):
                gdn_ref[at, h * own : (h + 1) * own] = mm_tn(g, factor(1, h)).astype(BF)
            gup_ref[:, at] = mm_tn(near_x, du).astype(BF)
            gnear_ref[:, at] = mm_tn(far_x, du).astype(BF)
            x = copy(gnear_ref.at[:, at], gfar_ref.at[:, at], u_send.at[c], u_recv.at[c], partner)
            x.start()
            pending.append(x.wait)

        chunks = list(range(ff_own // size))

    cross = got_ref.shape[0]
    small_ops = small_start(0, small)
    for level in range(levels):
        if level > 0:
            gather_finish(gathers)
            gathers = gather_stage(last - 1 - level) if level < last else []
        for t in range(plan.streams):
            reduce_finish(t, level, running[t])
            running[t] = reduce_start(t, level + 1) if level < last else spread_start(t, last)
        small = small_finish(level, small_ops)
        small_ops = small_start(level + 1, small) if level < last else []
    total_ref[...] = small
    for wait in pending:
        wait()
    pending.clear()
    if fused:
        for f in fetches[2:]:
            f.wait()
        for h in range(2):
            dbias_ref[h : h + 1] = jnp.sum(factor(1, h).astype(F32), axis=0, keepdims=True)
    for level in range(last, -1, -1):
        for t in range(plan.streams):
            if chunks and t % 2 == 0:
                chunk(chunks.pop(0))
            for c in running[t]:
                c.wait()
            if level > 0:
                running[t] = spread_start(t, level - 1)
            elif t * span < cross:
                rows_x = pl.ds(t * span, min(span, cross - t * span))
                x = copy(res_ref.at[rows_x], got_ref.at[rows_x], x_send.at[t], x_recv.at[t], partner)
                x.start()
                pending.append(x.wait)
    while chunks:
        chunk(chunks.pop(0))
    for wait in pending:
        wait()


def ffn_kernel(
    gath_ref, wup_m, wup_o, wdn_m, upb_ref,
    gdn_ref, gup_ref, gsend_ref, bias_ref, dbias_ref,
    down_ref, near_ref, far_ref,
):
    s = lax.axis_index("seq")
    step, steps = pl.program_id(0), pl.num_programs(0)
    own = gath_ref.shape[3]
    ff_own = wdn_m.shape[0]
    size = 512 if ff_own % 512 == 0 else ff_own
    sides = pl.ds(s, 1), pl.ds(1 - s, 1)

    @pl.when(step == 0)
    def _():
        for ref in (down_ref, near_ref, far_ref, bias_ref, dbias_ref):
            ref[...] = jnp.zeros_like(ref)

    for h in range(2):
        dbias_ref[h : h + 1] += jnp.sum(gath_ref[1, h].astype(F32), axis=0, keepdims=True)
    for c in range(ff_own // size):
        cols = lanes(s * ff_own + c * size, size)
        at = slice(c * size, (c + 1) * size)
        u = mm(gath_ref[0, sides[0]][0], wup_m[:, cols])
        u = u + mm(gath_ref[0, sides[1]][0], wup_o[:, cols]) + upb_ref[:, cols]
        phi = gelu_cdf(u)
        g = (u * phi).astype(BF)
        dg = mm_nt(gath_ref[1, 0], wdn_m[at, :own]) + mm_nt(gath_ref[1, 1], wdn_m[at, own:])
        du = (dg * gelu_slope(u, phi)).astype(BF)
        bias_ref[:, at] += jnp.sum(du.astype(F32), axis=0, keepdims=True)
        for h in range(2):
            down_ref[at, h * own : (h + 1) * own] += mm_tn(g, gath_ref[1, h])
        near_ref[:, at] += mm_tn(gath_ref[0, sides[0]][0], du)
        far_ref[:, at] += mm_tn(gath_ref[0, sides[1]][0], du)

    @pl.when(step == steps - 1)
    def _():
        gsend_ref[...] = far_ref[...].astype(BF)
        gdn_ref[...] = down_ref[...].astype(BF)
        gup_ref[...] = near_ref[...].astype(BF)


def final_kernel(
    own_ref, out_ref, got_ref, gup_ref, gfar_ref, gdn_ref, dkeep_ref, drecv_ref,
    gqkv_out, gout_out, gup_out, gdn_out, gtok_out,
):
    s = lax.axis_index("seq")
    own = got_ref.shape[2]
    width, ff_own = 2 * own, gup_ref.shape[1]
    for j in range(3):
        gqkv_out[:, lanes(j * width + s * own, own)] = own_ref[j].astype(F32)
        gqkv_out[:, lanes(j * width + (1 - s) * own, own)] = got_ref[j].astype(F32)
    for h in range(2):
        gout_out[:, h * own : (h + 1) * own] = out_ref[h].astype(F32)
    gup_out[:, lanes(s * ff_own, ff_own)] = gup_ref[...].astype(F32)
    gup_out[:, lanes((1 - s) * ff_own, ff_own)] = gfar_ref[...].astype(F32)
    gdn_out[...] = gdn_ref[...].astype(F32)
    gtok_out[...] = (dkeep_ref[...] + drecv_ref[...].astype(F32)).astype(BF)


def shape(dims, kind=BF):
    return jax.ShapeDtypeStruct(dims, kind)


def local_call(kernel, outs, scratch=(), scalars=0, args=0):
    extra = {}
    if scalars:
        extra["in_specs"] = [pl.BlockSpec(memory_space=pltpu.SMEM)] * scalars + [
            pl.BlockSpec(memory_space=pltpu.VMEM)
        ] * (args - scalars)
    return pl.pallas_call(
        kernel,
        out_shape=outs,
        scratch_shapes=scratch,
        compiler_params=pltpu.CompilerParams(vmem_limit_bytes=VMEM_LIMIT),
        **extra,
    )


def body(
    mesh, tokens, w_qkv, q_bias, v_bias, w_out, out_bias, attn_gain, attn_shift, w_up, up_bias,
    w_down, down_bias, ffn_gain, ffn_shift, seq_len, grad_pos, grad_count, out_grad,
):
    half, width = tokens.shape[1:]
    own, ff_own = w_qkv.shape[0], w_down.shape[0]
    length, slots, ff = 2 * half, grad_pos.shape[1], 2 * ff_own
    plan = Plan(mesh, 8 * own)
    n = plan.n
    s = lax.axis_index("seq")
    swap = lambda x: lax.ppermute(x, "seq", [(0, 1), (1, 0)])
    tm = tokens[0]
    cols = jnp.concatenate(
        [lax.dynamic_slice_in_dim(w_qkv, j * width + (1 - s) * own, own, 1) for j in range(3)], axis=1
    )
    to, wqkv_o = swap(tm), swap(cols)
    wout_o, wup_o, wdn_o = swap(w_out), swap(w_up), swap(w_down)
    vec = jnp.stack(
        [out_bias, attn_gain, attn_shift, down_bias, ffn_gain, ffn_shift, q_bias, v_bias]
    )
    upb = up_bias.reshape(1, ff)
    row = jnp.arange(length, dtype=jnp.int32)
    pos = jnp.where(row < half, row + s * half, row - half + (1 - s) * half)
    live = jnp.arange(slots)[:, None] < grad_count[0]
    hot = ((grad_pos[0][:, None] == pos[None, :]) & live).astype(BF)
    msk = (pos < seq_len[0]).astype(F32)[None]

    qkv, keep, send, tr, crow = local_call(
        attend_kernel,
        [shape((length, 3 * own)), shape((half + slots, own)), shape((half + slots, own)),
         shape((slots, width)), shape((slots, own))],
        [pltpu.VMEM((length, own), BF)],
    )(tm, to, w_qkv, wqkv_o, vec, hot, msk)
    recv = swap(send)
    out, fac, dat, dh1, dctx, sums = local_call(
        feed_kernel,
        [shape((half, width)), shape((2, 2, slots, own)), shape((slots, width)),
         shape((slots, width), F32), shape((slots, own)), shape((8, width), F32)],
        [pltpu.VMEM((half + slots, width), BF), pltpu.VMEM((half + slots, width), F32),
         pltpu.VMEM((slots, ff), F32), pltpu.VMEM((half + slots, width), F32),
         pltpu.VMEM((slots, width), F32)],
        scalars=1, args=14,
    )(grad_count, keep, recv, tm, tr, w_out, wout_o, w_up, wup_o, w_down, wdn_o, vec, upb, out_grad[0])
    dma = pltpu.SemaphoreType.DMA
    depth, widest = len(plan.orders[0]), max(size for size, _ in plan.orders[0]) - 1
    slots_small = sum(size for size, _ in plan.orders[0])
    cross, rows = 3 * own, n * slots
    fused = rows <= 1280
    sizes = tuple(size for size, _ in plan.orders[0])
    keep_ff = (lambda *dims: dims) if fused else (lambda *dims: (16, 128))
    vmem, hbm = pl.BlockSpec(memory_space=pltpu.VMEM), pl.BlockSpec(memory_space=pl.ANY)
    res, got, gath, total, dkeep, drecv, gdn, gup, gfar, ubias, dbias = pl.pallas_call(
        functools.partial(reduce_kernel, plan, fused),
        in_specs=[vmem] * 12 + [hbm] * 5 + [vmem],
        out_shape=[shape((plan.rows, own)), shape((cross, own)), shape((2, 2, *sizes, slots, own)),
                   shape((8, own), F32), shape((half, width), F32), shape((half, width)),
                   shape(keep_ff(ff_own, width)), shape(keep_ff(own, ff_own)),
                   shape(keep_ff(own, ff_own)), shape((1, ff_own), F32), shape((2, own), F32)],
        scratch_shapes=[
            pltpu.VMEM((plan.rows, own), BF), pltpu.VMEM((plan.rows, own), BF),
            pltpu.VMEM((plan.rows, own), BF), pltpu.VMEM((slots_small, 8, own), F32),
            pltpu.VMEM((length, 3 * own), BF), pltpu.VMEM((length, width), F32),
            pltpu.VMEM((half, width), BF), pltpu.VMEM(keep_ff(own, ff_own), BF),
            pltpu.VMEM((own, 3 * width), BF), pltpu.VMEM((own, 3 * own), BF),
            pltpu.VMEM(keep_ff(own, ff), BF), pltpu.VMEM(keep_ff(own, ff), BF),
            pltpu.VMEM(keep_ff(ff_own, width), BF),
            dma((plan.streams, plan.copies)), dma((plan.streams, plan.copies)),
            dma((plan.streams, plan.copies)), dma((plan.streams, plan.copies)),
            dma((2, depth, widest)), dma((2, depth, widest)),
            dma((2, depth, widest)), dma((2, depth, widest)),
            dma((2,)), dma((2,)),
            dma((slots_small,)), dma((slots_small,)),
            dma((plan.streams,)), dma((plan.streams,)),
            dma, dma, dma((8,)), dma((8,)), dma((5,)),
        ],
        compiler_params=pltpu.CompilerParams(
            collective_id=0, has_side_effects=True, vmem_limit_bytes=VMEM_LIMIT
        ),
    )(fac, qkv, hot, msk, dctx, tm, to, tr, crow, dat, dh1, sums, w_qkv, wqkv_o, w_up, wup_o, w_down, upb)

    if not fused:
        tile = 1280 if rows % 1280 == 0 else slots
        fixed = lambda *dims: pl.BlockSpec(dims, lambda i: (0,) * len(dims), pipeline_mode=pl.Buffered(1))
        gdn, gup, gsend, ubias, dbias = pl.pallas_call(
            ffn_kernel,
            grid=(rows // tile,),
            in_specs=[pl.BlockSpec((2, 2, tile, own), lambda i: (0, 0, i, 0)), fixed(own, ff),
                      fixed(own, ff), fixed(ff_own, width), fixed(1, ff)],
            out_specs=[fixed(ff_own, width), fixed(own, ff_own), fixed(own, ff_own),
                       fixed(1, ff_own), fixed(2, own)],
            out_shape=[shape((ff_own, width)), shape((own, ff_own)), shape((own, ff_own)),
                       shape((1, ff_own), F32), shape((2, own), F32)],
            scratch_shapes=[pltpu.VMEM((ff_own, width), F32), pltpu.VMEM((own, ff_own), F32),
                            pltpu.VMEM((own, ff_own), F32)],
            compiler_params=pltpu.CompilerParams(vmem_limit_bytes=VMEM_LIMIT),
        )(gath.reshape(2, 2, rows, own), w_up, wup_o, w_down, upb)
        gfar = swap(gsend)
    cut = 4 if own % 64 == 0 else 1
    block = own // cut
    res = res[: 8 * own].reshape(8, own, own)
    flat = lambda r, c: pl.BlockSpec((r, c), lambda i: (i, 0))
    gqkv, gout, gup, gdn, gtok = pl.pallas_call(
        final_kernel,
        grid=(cut,),
        in_specs=[pl.BlockSpec((3, block, own), lambda i: (1, i, 0)),
                  pl.BlockSpec((2, block, own), lambda i: (3, i, 0)),
                  pl.BlockSpec((3, block, own), lambda i: (0, i, 0)),
                  flat(block, ff_own), flat(block, ff_own), flat(ff_own // cut, width),
                  flat(half // cut, width), flat(half // cut, width)],
        out_specs=[flat(block, 3 * width), flat(block, width), flat(block, ff),
                   flat(ff_own // cut, width), flat(half // cut, width)],
        out_shape=[shape((own, 3 * width), F32), shape((own, width), F32), shape((own, ff), F32),
                   shape((ff_own, width), F32), shape((half, width))],
        compiler_params=pltpu.CompilerParams(vmem_limit_bytes=VMEM_LIMIT),
    )(res, res, got.reshape(3, own, own), gup, gfar, gdn, dkeep, drecv)
    return (
        out[None], gtok[None], gqkv, total[0], total[1], gout, total[2], total[3], total[4], gup,
        ubias[0], gdn, lax.dynamic_index_in_dim(dbias, s, 0, keepdims=False), total[5], total[6],
    )


def solution(mesh):
    specs = dict(
        in_specs=(
            P("batch", "seq", None), P("seq", None), P(), P(), P("seq", None), P(), P(), P(),
            P("seq", None), P(), P("seq", None), P(), P(), P(), P("batch"), P("batch", None),
            P("batch"), P("batch", None, None),
        ),
        out_specs=(
            P("batch", "seq", None), P("batch", "seq", None), P("seq", None), P("seq"), P("seq"),
            P("seq", None), P("seq"), P("seq"), P("seq"), P("seq", None), P("seq"),
            P("seq", None), P("seq"), P("seq"), P("seq"),
        ),
    )
    return jax.shard_map(functools.partial(body, mesh), mesh=mesh, check_vma=False, **specs)
```

```python
import functools
import math

import jax
import jax.numpy as jnp
import numpy as np
from jax import lax
from jax.experimental import pallas as pl
from jax.experimental.pallas import tpu as pltpu
from jax.sharding import PartitionSpec as P

HEAD_DIM = 64
NORM_EPS = 1e-05
MASKED = -1000000000.0
BF = jnp.bfloat16
F32 = jnp.float32
MESH = pl.DeviceIdType.MESH
VMEM_LIMIT = 63 * 1024 * 1024


def mm(a, b):
    return lax.dot_general(a, b, (((1,), (0,)), ((), ())), preferred_element_type=F32)


def mm_nt(a, b):
    return lax.dot_general(a, b, (((1,), (1,)), ((), ())), preferred_element_type=F32)


def mm_tn(a, b):
    return lax.dot_general(a, b, (((0,), (0,)), ((), ())), preferred_element_type=F32)


def lanes(start, size):
    return pl.ds(pl.multiple_of(start, 128), size)


def gelu_cdf(u):
    return 0.5 + 0.5 * lax.erf(u * (2.0**-0.5))


def gelu_slope(u, phi):
    return phi + u * ((2.0 * math.pi) ** -0.5) * jnp.exp(-0.5 * u * u)


def norm_stats(x):
    center = x - jnp.mean(x, axis=-1, keepdims=True)
    inverse = lax.rsqrt(jnp.mean(center * center, axis=-1, keepdims=True) + NORM_EPS)
    return center * inverse, inverse


def norm_back(up, unit, inverse, gain):
    e = up * gain
    return inverse * (
        e - jnp.mean(e, axis=-1, keepdims=True) - unit * jnp.mean(e * unit, axis=-1, keepdims=True)
    )


def pick(value, which, own):
    return jnp.where(which == 0, value[:, :own], value[:, own:])


class Plan:
    def __init__(self, mesh, rows):
        axis = mesh.axis_names.index("batch")
        line = np.moveaxis(mesh.devices, axis, 0)
        line = line.reshape(line.shape[0], -1)[:, 0]
        n = len(line)
        self.n = n
        dims = []
        try:
            coords = [tuple(d.coords) for d in line]
            for d in range(3):
                size = len({c[d] for c in coords})
                if size > 1:
                    first = coords[0]
                    stride = next(
                        i
                        for i, c in enumerate(coords)
                        if c[d] != first[d] and all(c[e] == first[e] for e in range(3) if e != d)
                    )
                    dims.append((size, stride))
            good = all(
                c[d] >= 0 for c in coords for d in range(3)
            ) and math.prod(size for size, _ in dims) == n
            if not good:
                dims = []
        except (AttributeError, StopIteration):
            dims = []
        if not dims:
            rest, stride = n, 1
            while rest > 1:
                dims.append((2 if rest % 2 == 0 else rest, stride))
                stride *= dims[-1][0]
                rest //= dims[-1][0]
        dims.sort()
        self.orders = [dims]
        if len(dims) > 1:
            self.orders.append([dims[1], dims[0]] + dims[2:])
        halves = []
        for size, stride in dims:
            if size > 2 and size & (size - 1) == 0:
                while size > 1:
                    halves.append((2, stride))
                    size, stride = size // 2, stride * 2
            else:
                halves.append((size, stride))
        first = 2 if len(dims) > 1 and dims[0][0] == dims[1][0] == 2 else 0
        plain = halves
        turned = [halves[1], halves[0]] + halves[2:] if first else halves
        deep = halves[2:] + [halves[1], halves[0]] if first and len(halves) > 3 else plain
        self.lanes = [plain, turned, plain, deep]
        self.peers = [(size, stride, o) for size, stride in dims for o in range(1, size)]
        unit = 16 * n
        streams = max(2, min(4, rows // unit))
        streams += streams % 2
        self.piece = -(-rows // (streams * unit)) * 16
        self.streams = streams
        self.rows = streams * n * self.piece
        self.copies = sum(size - 1 for size, _ in halves)


def coordinate(me, size, stride):
    return lax.rem(lax.div(me, stride), size)


def peer_of(me, size, stride, offset):
    here = coordinate(me, size, stride)
    there = lax.rem(here + offset, size)
    return me + (there - here) * stride, there


def layer_kernel(
    plan, fused,
    len_ref, count_ref, tm_ref, gp_ref, grad_ref, ob_ref, g1_ref, s1_ref, db_ref, g2_ref, s2_ref, qb_ref,
    vb_ref, upb_ref, wq_any, wo_any, wu_any, wd_any,
    out_out, res_out, got_out, total_ref, dkeep_out, drecv_out, gdn_out, gup_out, gfar_out,
    ubias_ref, dbias_ref, gath_ref, wuo_ref,
    out_ref, res_ref, dkeep_ref, gdn_ref, gup_ref,
    to_ref, wqm_ref, wqo_ref, wom_ref, woo_ref, wum_ref, wdm_ref, wdo_ref, qkv_ref, ctx_ref, crow_ref,
    crecv_ref, ab_ref, acc_ref, slope_ref, da_ref, load_ref, buf_ref, in_ref, sm_ref, dp_ref, part_ref,
    dsend_ref, gnear_ref, fac_ref,
    rs_send, rs_recv, ag_send, ag_recv, fa_send, fa_recv, fw_send, fw_recv, ow_send, ow_recv,
    sm_send, sm_recv, x_send, x_recv, d_send, d_recv, u_send, u_recv, c_send, c_recv, w_send, w_recv, w_sem, o_sem,
):
    me = lax.axis_index("batch")
    s = lax.axis_index("seq")
    n, piece = plan.n, plan.piece
    half, width = tm_ref.shape
    own = width // 2
    length = 2 * half
    slots = grad_ref.shape[0]
    ff_own = wdm_ref.shape[0]
    mine, other = lanes(s * own, own), lanes((1 - s) * own, own)
    partner = {"seq": 1 - s}

    fetches = [
        pltpu.make_async_copy(a, b, w_sem.at[i])
        for i, (a, b) in enumerate(
            [(wq_any, wqm_ref), (wo_any, wom_ref), (wu_any, wum_ref), (wd_any, wdm_ref)]
        )
    ]
    for f in fetches:
        f.start()
    barrier = pltpu.get_barrier_semaphore()
    for size, stride, o in plan.peers:
        to, _ = peer_of(me, size, stride, o)
        pl.semaphore_signal(barrier, inc=1, device_id={"batch": to}, device_id_type=MESH)
    pl.semaphore_signal(barrier, inc=1, device_id=partner, device_id_type=MESH)
    pl.semaphore_wait(barrier, len(plan.peers) + 1)

    def copy(src, dst, send, recv, where):
        return pltpu.make_async_remote_copy(
            src_ref=src, dst_ref=dst, send_sem=send, recv_sem=recv, device_id=where,
            device_id_type=MESH,
        )

    pending = []
    trades = []

    def keep_out(i, src, dst):
        c = pltpu.make_async_copy(src, dst, o_sem.at[i])
        c.start()
        pending.append(c.wait)


    def trade(i, src, dst):
        c = copy(src, dst, w_send.at[i], w_recv.at[i], partner)
        c.start()
        trades.append(c)

    trade(0, tm_ref, to_ref)
    for j in range(3):
        trade(1 + j, wq_any.at[:, lanes(j * width + (1 - s) * own, own)], wqo_ref.at[:, pl.ds(j * own, own)])
    trade(4, wo_any, woo_ref)
    trade(5, wu_any, wuo_ref)
    trade(6, wd_any, wdo_ref)

    spot = lax.broadcasted_iota(jnp.int32, (1, length), 1)
    pos = jnp.where(spot < half, spot + s * half, spot - half + (1 - s) * half)
    valid = pos < len_ref[0]
    square = (slots, slots)
    eye = lax.broadcasted_iota(jnp.int32, square, 0) == lax.broadcasted_iota(jnp.int32, square, 1)
    column = jnp.sum(jnp.where(eye, gp_ref[...].astype(F32), 0.0), axis=1, keepdims=True)
    used = lax.broadcasted_iota(jnp.int32, (slots, 1), 0) < count_ref[0]
    hit = (column == pos.astype(F32)) & used
    hot = jnp.where(hit, 1.0, 0.0).astype(BF)

    def line(ref):
        return ref[...].reshape(1, ref.shape[0])

    fetches[0].wait()
    for c in trades[:4]:
        c.wait()
    bias = {0: qb_ref, 2: vb_ref}
    for j in range(3):
        w_m = wqm_ref[:, lanes(j * width + s * own, own)]
        w_o = wqo_ref[:, j * own : (j + 1) * own]
        for b, rows in enumerate((tm_ref, to_ref)):
            acc = mm(rows[:, mine], w_m) + mm(rows[:, other], w_o)
            if j in bias:
                acc = acc + bias[j][mine].reshape(1, own)
            qkv_ref[b * half : (b + 1) * half, j * own : (j + 1) * own] = acc.astype(BF)
    t_rows = (mm(hot[:, :half], tm_ref[...]) + mm(hot[:, half:], to_ref[...])).astype(BF)
    ones = jnp.ones((length, 128), BF)
    low = lax.broadcasted_iota(jnp.int32, (1, 128), 1) < HEAD_DIM
    sent = []
    for pair in range(own // 128):
        at = pair * 128
        keys = qkv_ref[:, own + at : own + at + 128]
        vals = jnp.concatenate([qkv_ref[:, 2 * own + at : 2 * own + at + 128], ones], axis=1)
        for b in (1, 0):
            q2 = qkv_ref[b * half : (b + 1) * half, at : at + 128] * jnp.array(HEAD_DIM**-0.5, BF)
            parts = []
            for e in range(2):
                q = jnp.where(low if e == 0 else ~low, q2, jnp.zeros_like(q2))
                scores = jnp.where(valid, mm_nt(q, keys), MASKED)
                top = jnp.max(scores, axis=-1, keepdims=True)
                weights = jnp.exp(scores - top).astype(BF)
                mixed = mm(weights, vals)
                parts.append(mixed[:, :128] / mixed[:, 128:])
            ctx_ref[b * half : (b + 1) * half, at : at + 128] = jnp.where(
                low, parts[0], parts[1]
            ).astype(BF)
            if b == 1:
                block = pl.ds(at, 128)
                c = copy(
                    ctx_ref.at[pl.ds(half, half), block], crecv_ref.at[pl.ds(0, half), block],
                    c_send.at[pair], c_recv.at[pair], partner,
                )
                c.start()
                sent.append(c)
    crow_ref[...] = mm(hot, ctx_ref[...]).astype(BF)
    c = copy(crow_ref, crecv_ref.at[pl.ds(half, slots)], c_send.at[3], c_recv.at[3], partner)
    c.start()
    sent.append(c)

    def place(order):
        spots, base, span = [], jnp.int32(0), n
        for size, stride in order:
            span //= size
            spots.append((base, span))
            base = base + coordinate(me, size, stride) * span
        return spots, base

    places = [place(order) for order in plan.orders]

    dims = plan.orders[0]
    levels = len(dims)
    last = levels - 1
    span = n * piece

    def window(kind, part, done, moved=None, there=None):
        spots = []
        for dim in dims:
            if dim == moved:
                spots.append(pl.ds(there, 1))
            elif dim in done:
                spots.append(pl.ds(0, dim[0]))
            else:
                spots.append(pl.ds(coordinate(me, *dim), 1))
        return gath_ref.at[(kind, s, *spots, pl.ds(*part))]

    unit = (1,) * levels
    cut = -(-slots // 32) * 16
    parts_of = [(0, cut), (cut, slots - cut)] if cut < slots else [(0, slots)]

    def gather_stage(kind, level):
        started = []
        for i, part in enumerate(parts_of):
            order = plan.orders[i % len(places)]
            dim, done = order[level], order[level + 1 :]
            size, stride = dim
            here = coordinate(me, size, stride)
            for o in range(1, size):
                to, _ = peer_of(me, size, stride, o)
                sem = (kind, i, level, o - 1)
                block = window(kind, part, done)
                src = fac_ref.at[(kind, *[pl.ds(0, 1)] * levels, pl.ds(*part))] if level == last else block
                c = copy(src, block, fa_send.at[sem], fa_recv.at[sem], {"batch": to})
                c.start()
                back = lax.rem(here + size - o, size)
                started.append((c, sem, window(kind, part, done, dim, back)))
        return started

    def gather_begin(kind, value):
        fac_ref[kind] = value.reshape(unit + value.shape)
        everything = (0, slots)
        if fused:
            here = tuple(pl.ds(coordinate(me, *dim), 1) for dim in dims)
            gath_ref[(pl.ds(kind, 1), pl.ds(s, 1), *here)] = value.reshape((1, 1) + unit + value.shape)
        else:
            keep = pltpu.make_async_copy(fac_ref.at[kind], window(kind, everything, ()), w_sem.at[4 + kind])
            keep.start()
            keep.wait()
        gathers[kind] = (last, gather_stage(kind, last))
        c = copy(fac_ref.at[kind], window(kind, everything, ()), ow_send.at[kind], ow_recv.at[kind], partner)
        c.start()
        pending.append(c.wait)

    gathers = {}

    def gather_step(kind):
        level, started = gathers[kind]
        if level < 0:
            return
        for c, _, _ in started:
            c.wait_recv()
        gathers[kind] = (level - 1, gather_stage(kind, level - 1) if level > 0 else [])
        for c, sem, theirs in started:
            f = copy(theirs, theirs, fw_send.at[sem], fw_recv.at[sem], partner)
            f.start()
            pending.append(c.wait_send)
            pending.append(f.wait)

    tracks = [place(order) for order in plan.lanes]
    depth = len(plan.lanes[0])
    bottom = depth - 1

    def reduce_start(stream, level):
        order = plan.lanes[stream % 4]
        base, span = tracks[stream % 4][0][level]
        size, stride = order[level]
        off = stream * n * piece
        ops = []
        count = sum(z - 1 for z, _ in order[:level])
        for o in range(1, size):
            to, there = peer_of(me, size, stride, o)
            src = load_ref if level == 0 else buf_ref
            at = pl.ds(pl.multiple_of(off + (base + there * span) * piece, 16), span * piece)
            slot = pl.ds(in_base(stream, level) + (o - 1) * span * piece, span * piece)
            sem = (stream, count + o - 1)
            c = copy(src.at[at], in_ref.at[slot], rs_send.at[sem], rs_recv.at[sem], {"batch": to})
            c.start()
            ops.append(c)
        return ops

    def in_base(stream, level):
        order = plan.lanes[stream % 4]
        rows, span = 0, n
        for size, _ in order[:level]:
            span //= size
            rows += (size - 1) * span
        return (stream * n + rows) * piece

    def reduce_finish(stream, level, ops):
        order = plan.lanes[stream % 4]
        base, span = tracks[stream % 4][0][level]
        size, stride = order[level]
        off = stream * n * piece
        for c in ops:
            c.wait()
        here = coordinate(me, size, stride)
        at = pl.ds(pl.multiple_of(off + (base + here * span) * piece, 16), span * piece)
        src = load_ref if level == 0 else buf_ref
        acc = src[at].astype(F32)
        for o in range(1, size):
            slot = pl.ds(in_base(stream, level) + (o - 1) * span * piece, span * piece)
            acc = acc + in_ref[slot].astype(F32)
        dst = res_ref if level == bottom else buf_ref
        dst[at] = acc.astype(BF)

    def spread_start(stream, level):
        order = plan.lanes[stream % 4]
        base, span = tracks[stream % 4][0][level]
        size, stride = order[level]
        off = stream * n * piece
        here = coordinate(me, size, stride)
        at = pl.ds(pl.multiple_of(off + (base + here * span) * piece, 16), span * piece)
        count = sum(z - 1 for z, _ in order[:level])
        ops = []
        for o in range(1, size):
            to, _ = peer_of(me, size, stride, o)
            sem = (stream, count + o - 1)
            c = copy(res_ref.at[at], res_ref.at[at], ag_send.at[sem], ag_recv.at[sem], {"batch": to})
            c.start()
            ops.append(c)
        return ops

    def small_start(level, value):
        size, stride = plan.orders[0][level]
        here = coordinate(me, size, stride)
        first = sum(z for z, _ in plan.orders[0][:level])
        sm_ref[pl.ds(first + here, 1)] = value[None]
        ops = []
        for o in range(1, size):
            to, _ = peer_of(me, size, stride, o)
            sem = first + o
            slot = pl.ds(first + here, 1)
            c = copy(sm_ref.at[slot], sm_ref.at[slot], sm_send.at[sem], sm_recv.at[sem], {"batch": to})
            c.start()
            ops.append(c)
        return ops

    def small_finish(level, ops):
        for c in ops:
            c.wait()
        size, _ = plan.orders[0][level]
        first = sum(z for z, _ in plan.orders[0][:level])
        acc = sm_ref[first]
        for o in range(1, size):
            acc = acc + sm_ref[first + o]
        return acc


    gain1, gain2 = line(g1_ref), line(g2_ref)
    fetches[1].wait()
    for c in [trades[4]] + sent:
        c.wait()
    near_c = jnp.concatenate([ctx_ref[:half], crow_ref[...]], axis=0)
    attn = mm(near_c, wom_ref[...]) + mm(crecv_ref[...], woo_ref[...]) + line(ob_ref)
    tok = jnp.concatenate([tm_ref[...], t_rows], axis=0).astype(F32)
    unit1, inv1 = norm_stats(tok + attn)
    a = unit1 * gain1 + line(s1_ref)
    ab_ref[...] = a.astype(BF)
    unit1_r, inv1_r = unit1[half:], inv1[half:]
    acc_ref[...] = a + line(db_ref)
    gather_begin(0, ab_ref[half:, mine])
    for f in fetches[2:]:
        f.wait()
    trades[5].wait()
    step = ff_own // 2
    sides = ((wdm_ref, s * ff_own), (wdo_ref, (1 - s) * ff_own))
    for part, (down, base) in enumerate(sides):
        if part == 1:
            trades[6].wait()
        for c in range(ff_own // step):
            cols = lanes(base + c * step, step)
            u = mm(ab_ref[:, mine], wum_ref[:, cols]) + mm(ab_ref[:, other], wuo_ref[:, cols])
            u = u + upb_ref[cols].reshape(1, step)
            phi = gelu_cdf(u)
            g = (u * phi).astype(BF)
            k = part * ff_own + c * step
            slope_ref[:, k : k + step] = gelu_slope(u[half:], phi[half:])
            acc_ref[...] += mm(g, down[c * step : (c + 1) * step])
    unit2, inv2 = norm_stats(acc_ref[...])
    unit2_r, inv2_r = unit2[half:], inv2[half:]
    dy = jnp.where(used, grad_ref[...].astype(F32), 0.0)
    dh2 = norm_back(dy, unit2_r, inv2_r, gain2)
    df = dh2.astype(BF)
    da_ref[...] = dh2
    gather_begin(1, pick(df, s, own))
    gather_step(0)
    out_ref[...] = (unit2[:half] * gain2 + line(s2_ref)).astype(BF)
    keep_out(0, out_ref, out_out)
    da_m = jnp.zeros((slots, own), F32)
    da_o = jnp.zeros((slots, own), F32)
    for part, (down, base) in enumerate(sides):
        for c in range(ff_own // step):
            cols = lanes(base + c * step, step)
            k = part * ff_own + c * step
            dg = mm_nt(df, down[c * step : (c + 1) * step])
            du = (dg * slope_ref[:, k : k + step]).astype(BF)
            da_m = da_m + mm_nt(du, wum_ref[:, cols])
            da_o = da_o + mm_nt(du, wuo_ref[:, cols])
    da_ref[:, mine] += da_m
    da_ref[:, other] += da_o
    da = da_ref[...]
    dh1 = norm_back(da, unit1_r, inv1_r, gain1)
    dat = dh1.astype(BF)
    d_ctx = mm_nt(dat, wom_ref[...]).astype(BF)
    gather_step(0)

    running = {}
    ready = set()

    def finished(first, end):
        ready.update(range(first, end))
        for t in range(plan.streams):
            rows = range(t * span // own, -(-min((t + 1) * span, 8 * own) // own))
            if t not in running and all(r in ready for r in rows):
                running[t] = reduce_start(t, 0)

    if load_ref.shape[0] > 8 * own:
        load_ref[8 * own :] = jnp.zeros((load_ref.shape[0] - 8 * own, own), BF)
    for h in range(2):
        g = mm_tn(crow_ref[...], dat[:, h * own : (h + 1) * own])
        load_ref[(6 + h) * own : (7 + h) * own] = g.astype(BF)
    finished(6, 8)
    scale = HEAD_DIM**-0.5
    q_rows = (mm(hot, qkv_ref[:, :own]) * scale).astype(BF)
    dq = []
    for pair in range(own // 128):
        at = pair * 128
        keys = qkv_ref[:, own + at : own + at + 128]
        vals = qkv_ref[:, 2 * own + at : 2 * own + at + 128]
        q2, c2 = q_rows[:, at : at + 128], d_ctx[:, at : at + 128]
        zero = jnp.zeros_like(q2)
        q4 = jnp.concatenate([jnp.where(low, q2, zero), jnp.where(low, zero, q2)], axis=0)
        c4 = jnp.concatenate([jnp.where(low, c2, zero), jnp.where(low, zero, c2)], axis=0)
        scores = jnp.where(valid, mm_nt(q4, keys), MASKED)
        probs = jnp.exp(scores - jnp.max(scores, axis=-1, keepdims=True))
        probs = probs / jnp.sum(probs, axis=-1, keepdims=True)
        dprobs = mm_nt(c4, vals)
        ds = probs * (dprobs - jnp.sum(probs * dprobs, axis=-1, keepdims=True))
        ds = ds.astype(BF)
        r = mm(ds, keys) * scale
        dq.append(jnp.where(low, r[:slots], r[slots:]).astype(BF))
        dp_ref[:, 3 * at : 3 * at + 128] = mm_tn(hot, dq[-1]).astype(BF)
        dp_ref[:, 3 * at + 128 : 3 * at + 256] = mm_tn(ds, q4).astype(BF)
        dp_ref[:, 3 * at + 256 : 3 * at + 384] = mm_tn(probs.astype(BF), c4).astype(BF)
        cols = slice(3 * at, 3 * at + 384)
        for side, feats in enumerate((other, mine)):
            g = mm_tn(tm_ref[:, feats], dp_ref[:half, cols]) + mm_tn(to_ref[:, feats], dp_ref[half:, cols])
            section = 2 * pair + side
            load_ref[section * own : (section + 1) * own] = g.astype(BF)
        finished(2 * pair, 2 * pair + 2)
        if pair == 0:
            gather_step(1)
    dq = jnp.concatenate(dq, axis=1)
    gather_step(0)
    gather_step(1)

    p_m = jnp.zeros((length, own), F32)
    p_o = jnp.zeros((length, own), F32)
    for pair in range(own // 128):
        for j in range(3):
            at = pair * 128
            d = dp_ref[:, 3 * at + j * 128 : 3 * at + (j + 1) * 128]
            p_m = p_m + mm_nt(d, wqm_ref[:, lanes(j * width + s * own + at, 128)])
            p_o = p_o + mm_nt(d, wqo_ref[:, j * own + at : j * own + at + 128])
    part_ref[:, mine] = p_m
    part_ref[:, other] = p_o
    dsend_ref[...] = part_ref[half:].astype(BF)
    c = copy(dsend_ref, drecv_out, d_send, d_recv, partner)
    c.start()
    pending.append(c.wait)
    high = dh1.astype(BF)
    rest = (dh1 - high.astype(F32)).astype(BF)
    near = hot[:, :half]
    dkeep_ref[...] = part_ref[:half] + mm_tn(near, high) + mm_tn(near, rest)
    keep_out(1, dkeep_ref, dkeep_out)
    total = lambda x: jnp.sum(x, axis=0, keepdims=True)
    part_ref[0:1] = total(dat.astype(F32))
    part_ref[1:2] = total(da * unit1_r)
    part_ref[2:3] = total(da)
    part_ref[3:4] = total(dy * unit2_r)
    part_ref[4:5] = total(dy)
    v_sums = [total(dp_ref[:, 384 * p + 256 : 384 * p + 384].astype(F32)) for p in range(own // 128)]
    sums = [total(dq.astype(F32)), jnp.concatenate(v_sums, axis=1)]
    sums.append(part_ref[0:5, mine])
    sums.append(jnp.zeros((1, own), F32))
    small = jnp.concatenate(sums, axis=0)

    pieces = iter(())
    if fused:
        size = 512 if ff_own % 512 == 0 else ff_own
        rows = n * slots

        def factor(kind, h):
            value = gath_ref[kind, h] if isinstance(h, int) else gath_ref[kind, pl.ds(h, 1)]
            return value.reshape(rows, own)

        def work():
            for h in range(2):
                dbias_ref[h : h + 1] = jnp.sum(factor(1, h).astype(F32), axis=0, keepdims=True)
            for c in range(ff_own // size):
                cols = lanes(s * ff_own + c * size, size)
                at = slice(c * size, (c + 1) * size)
                u = mm(factor(0, s), wum_ref[:, cols]) + mm(factor(0, 1 - s), wuo_ref[:, cols])
                u = u + upb_ref[cols].reshape(1, size)
                phi = gelu_cdf(u)
                g = (u * phi).astype(BF)
                slope = gelu_slope(u, phi)
                yield
                dg = mm_nt(factor(1, 0), wdm_ref[at, :own]) + mm_nt(factor(1, 1), wdm_ref[at, own:])
                du = (dg * slope).astype(BF)
                ubias_ref[:, at] = jnp.sum(du.astype(F32), axis=0, keepdims=True)
                yield
                for h in range(2):
                    gdn_ref[at, h * own : (h + 1) * own] = mm_tn(g, factor(1, h)).astype(BF)
                keep_out(2 + c, gdn_ref.at[at], gdn_out.at[at])
                yield
                gnear_ref[:, at] = mm_tn(factor(0, 1 - s), du).astype(BF)
                x = copy(gnear_ref.at[:, at], gfar_out.at[:, at], u_send.at[c], u_recv.at[c], partner)
                x.start()
                pending.append(x.wait)
                gup_ref[:, at] = mm_tn(factor(0, s), du).astype(BF)
                keep_out(8 + c, gup_ref.at[:, at], gup_out.at[:, at])
                yield

    def flush():
        for wait in pending:
            wait()
        pending.clear()

    cross = got_out.shape[0]
    small_ops = small_start(0, small)
    for level in range(depth):
        for t in range(plan.streams):
            if level > 0:
                next(pieces, None)
            reduce_finish(t, level, running[t])
            running[t] = reduce_start(t, level + 1) if level < bottom else spread_start(t, bottom)
        if level < levels:
            small = small_finish(level, small_ops)
            small_ops = small_start(level + 1, small) if level < last else []
        while level == 0 and gathers[1][0] >= 0:
            gather_step(1)
        if level == 0:
            flush()
            if fused:
                pieces = work()
    total_ref[...] = small
    for level in range(bottom, -1, -1):
        for t in range(plan.streams):
            next(pieces, None)
            for c in running[t]:
                c.wait()
            if level > 0:
                running[t] = spread_start(t, level - 1)
                continue
            rows_r = pl.ds(t * span, span)
            keep_out(14 + t, res_ref.at[rows_r], res_out.at[rows_r])
            for p in range(cross // own):
                if (2 * p * own + own - 1) // span == t:
                    x = copy(
                        res_ref.at[pl.ds(2 * p * own, own)], got_out.at[pl.ds(p * own, own)],
                        x_send.at[p], x_recv.at[p], partner,
                    )
                    x.start()
                    pending.append(x.wait)
    for _ in pieces:
        pass
    flush()


def ffn_kernel(
    gath_ref, wup_m, wup_o, wdn_m, upb_ref,
    gdn_ref, gup_ref, gsend_ref, bias_ref, dbias_ref,
    down_ref, near_ref, far_ref,
):
    s = lax.axis_index("seq")
    step, steps = pl.program_id(0), pl.num_programs(0)
    own = gath_ref.shape[3]
    ff_own = wdn_m.shape[0]
    size = 512 if ff_own % 512 == 0 else ff_own
    sides = pl.ds(s, 1), pl.ds(1 - s, 1)

    @pl.when(step == 0)
    def _():
        for ref in (down_ref, near_ref, far_ref, bias_ref, dbias_ref):
            ref[...] = jnp.zeros_like(ref)

    for h in range(2):
        dbias_ref[h : h + 1] += jnp.sum(gath_ref[1, h].astype(F32), axis=0, keepdims=True)
    for c in range(ff_own // size):
        cols = lanes(s * ff_own + c * size, size)
        at = slice(c * size, (c + 1) * size)
        u = mm(gath_ref[0, sides[0]][0], wup_m[:, cols])
        u = u + mm(gath_ref[0, sides[1]][0], wup_o[:, cols]) + upb_ref[:, cols]
        phi = gelu_cdf(u)
        g = (u * phi).astype(BF)
        dg = mm_nt(gath_ref[1, 0], wdn_m[at, :own]) + mm_nt(gath_ref[1, 1], wdn_m[at, own:])
        du = (dg * gelu_slope(u, phi)).astype(BF)
        bias_ref[:, at] += jnp.sum(du.astype(F32), axis=0, keepdims=True)
        for h in range(2):
            down_ref[at, h * own : (h + 1) * own] += mm_tn(g, gath_ref[1, h])
        near_ref[:, at] += mm_tn(gath_ref[0, sides[0]][0], du)
        far_ref[:, at] += mm_tn(gath_ref[0, sides[1]][0], du)

    @pl.when(step == steps - 1)
    def _():
        gsend_ref[...] = far_ref[...].astype(BF)
        gdn_ref[...] = down_ref[...].astype(BF)
        gup_ref[...] = near_ref[...].astype(BF)


def final_kernel(
    own_ref, out_ref, got_ref, gup_ref, gfar_ref, gdn_ref, dkeep_ref, drecv_ref, total_ref, ubias_ref,
    dbias_ref,
    gqkv_out, gout_out, gup_out, gdn_out, gtok_out, ub_out, db_out, *sum_outs,
):
    s = lax.axis_index("seq")
    own = got_ref.shape[2]
    width, ff_own = 2 * own, gup_ref.shape[1]
    for j in range(3):
        for p in range(own // 128):
            part = slice(j * 128, (j + 1) * 128)
            gqkv_out[:, lanes(j * width + s * own + p * 128, 128)] = own_ref[p, 1, :, part].astype(F32)
            gqkv_out[:, lanes(j * width + (1 - s) * own + p * 128, 128)] = got_ref[p, :, part].astype(F32)
    for h in range(2):
        gout_out[:, h * own : (h + 1) * own] = out_ref[h].astype(F32)
    gup_out[:, lanes(s * ff_own, ff_own)] = gup_ref[...].astype(F32)
    gup_out[:, lanes((1 - s) * ff_own, ff_own)] = gfar_ref[...].astype(F32)
    gdn_out[...] = gdn_ref[...].astype(F32)
    gtok_out[...] = (dkeep_ref[...] + drecv_ref[...].astype(F32)).astype(BF)
    ub_out[...] = ubias_ref[0]
    db_out[...] = jnp.where(s == 0, dbias_ref[0], dbias_ref[1])
    for i, ref in enumerate(sum_outs):
        ref[...] = total_ref[i]


def shape(dims, kind=BF):
    return jax.ShapeDtypeStruct(dims, kind)


def body(
    mesh, tokens, w_qkv, q_bias, v_bias, w_out, out_bias, attn_gain, attn_shift, w_up, up_bias,
    w_down, down_bias, ffn_gain, ffn_shift, seq_len, grad_pos, grad_count, out_grad,
):
    half, width = tokens.shape[1:]
    own, ff_own = w_qkv.shape[0], w_down.shape[0]
    length, slots, ff = 2 * half, grad_pos.shape[1], 2 * ff_own
    plan = Plan(mesh, 8 * own)
    n = plan.n
    dma = pltpu.SemaphoreType.DMA
    depth, widest = len(plan.orders[0]), max(size for size, _ in plan.orders[0]) - 1
    slots_small = sum(size for size, _ in plan.orders[0])
    cross, rows = 3 * own, n * slots
    fused = rows <= 1280
    sizes = tuple(size for size, _ in plan.orders[0])
    ones = (1,) * depth
    keep_ff = (lambda *dims: dims) if fused else (lambda *dims: (16, 128))
    vmem, hbm = pl.BlockSpec(memory_space=pltpu.VMEM), pl.BlockSpec(memory_space=pl.ANY)
    smem = pl.BlockSpec(memory_space=pltpu.SMEM)
    total_rows = half + slots
    extra = [shape((2, 2, *sizes, slots, own)), shape((own, ff))]
    out, res, got, total, dkeep, drecv, gdn, gup, gfar, ubias, dbias, *more = pl.pallas_call(
        functools.partial(layer_kernel, plan, fused),
        in_specs=[smem] * 2 + [vmem] * 12 + [hbm] * 4,
        out_specs=[hbm] * 3 + [vmem] + [hbm] * 5 + [vmem] * 2 + ([] if fused else [hbm, vmem]),
        out_shape=[shape((half, width)), shape((plan.rows, own)), shape((cross, own)),
                   shape((8, own), F32), shape((half, width), F32), shape((half, width)),
                   shape(keep_ff(ff_own, width)), shape(keep_ff(own, ff_own)),
                   shape(keep_ff(own, ff_own)), shape((1, ff_own), F32), shape((2, own), F32),
                   *([] if fused else extra)],
        scratch_shapes=[
            *([pltpu.VMEM(e.shape, e.dtype) for e in extra] if fused else []),
            pltpu.VMEM((half, width), BF), pltpu.VMEM((plan.rows, own), BF), pltpu.VMEM((half, width), F32),
            pltpu.VMEM(keep_ff(ff_own, width), BF), pltpu.VMEM(keep_ff(own, ff_own), BF),
            pltpu.VMEM((half, width), BF), pltpu.VMEM((own, 3 * width), BF),
            pltpu.VMEM((own, 3 * own), BF), pltpu.VMEM((own, width), BF), pltpu.VMEM((own, width), BF),
            pltpu.VMEM((own, ff), BF), pltpu.VMEM((ff_own, width), BF), pltpu.VMEM((ff_own, width), BF),
            pltpu.VMEM((length, 3 * own), BF), pltpu.VMEM((length, own), BF),
            pltpu.VMEM((slots, own), BF), pltpu.VMEM((total_rows, own), BF),
            pltpu.VMEM((total_rows, width), BF), pltpu.VMEM((total_rows, width), F32),
            pltpu.VMEM((slots, ff), F32), pltpu.VMEM((slots, width), F32),
            pltpu.VMEM((plan.rows, own), BF), pltpu.VMEM((plan.rows, own), BF),
            pltpu.VMEM((plan.rows, own), BF), pltpu.VMEM((slots_small, 8, own), F32),
            pltpu.VMEM((length, 3 * own), BF), pltpu.VMEM((length, width), F32),
            pltpu.VMEM((half, width), BF), pltpu.VMEM(keep_ff(own, ff_own), BF),
            pltpu.VMEM((2, *ones, slots, own), BF),
            dma((plan.streams, plan.copies)), dma((plan.streams, plan.copies)),
            dma((plan.streams, plan.copies)), dma((plan.streams, plan.copies)),
            dma((2, 2, depth, widest)), dma((2, 2, depth, widest)),
            dma((2, 2, depth, widest)), dma((2, 2, depth, widest)),
            dma((2,)), dma((2,)),
            dma((slots_small,)), dma((slots_small,)),
            dma((3,)), dma((3,)),
            dma, dma, dma((8,)), dma((8,)), dma((4,)), dma((4,)), dma((7,)), dma((7,)), dma((6,)), dma((14 + plan.streams,)),
        ],
        compiler_params=pltpu.CompilerParams(
            collective_id=0, has_side_effects=True, vmem_limit_bytes=VMEM_LIMIT
        ),
    )(seq_len, grad_count, tokens[0], grad_pos, out_grad[0], out_bias, attn_gain, attn_shift, down_bias,
      ffn_gain, ffn_shift, q_bias, v_bias, up_bias, w_qkv, w_out, w_up, w_down)

    if not fused:
        gath, wup_o = more
        tile = 1280 if rows % 1280 == 0 else slots
        fixed = lambda *dims: pl.BlockSpec(dims, lambda i: (0,) * len(dims), pipeline_mode=pl.Buffered(1))
        gdn, gup, gsend, ubias, dbias = pl.pallas_call(
            ffn_kernel,
            grid=(rows // tile,),
            in_specs=[pl.BlockSpec((2, 2, tile, own), lambda i: (0, 0, i, 0)), fixed(own, ff),
                      fixed(own, ff), fixed(ff_own, width), fixed(1, ff)],
            out_specs=[fixed(ff_own, width), fixed(own, ff_own), fixed(own, ff_own),
                       fixed(1, ff_own), fixed(2, own)],
            out_shape=[shape((ff_own, width)), shape((own, ff_own)), shape((own, ff_own)),
                       shape((1, ff_own), F32), shape((2, own), F32)],
            scratch_shapes=[pltpu.VMEM((ff_own, width), F32), pltpu.VMEM((own, ff_own), F32),
                            pltpu.VMEM((own, ff_own), F32)],
            compiler_params=pltpu.CompilerParams(vmem_limit_bytes=VMEM_LIMIT),
        )(gath.reshape(2, 2, rows, own), w_up, wup_o, w_down, up_bias.reshape(1, ff))
        gfar = lax.ppermute(gsend, "seq", [(0, 1), (1, 0)])
    cut = 4 if own % 64 == 0 else 1
    block = own // cut
    res = res[: 8 * own].reshape(8, own, own)
    flat = lambda r, c: pl.BlockSpec((r, c), lambda i: (i, 0))
    whole = lambda *dims: pl.BlockSpec(dims, lambda i: (0,) * len(dims))
    gqkv, gout, gup, gdn, gtok, ub, db, *sums = pl.pallas_call(
        final_kernel,
        grid=(cut,),
        in_specs=[pl.BlockSpec((3, 2, block, own), lambda i: (0, 0, i, 0)),
                  pl.BlockSpec((2, block, own), lambda i: (3, i, 0)),
                  pl.BlockSpec((3, block, own), lambda i: (0, i, 0)),
                  flat(block, ff_own), flat(block, ff_own), flat(ff_own // cut, width),
                  flat(half // cut, width), flat(half // cut, width), whole(8, own), whole(1, ff_own),
                  whole(2, own)],
        out_specs=[flat(block, 3 * width), flat(block, width), flat(block, ff),
                   flat(ff_own // cut, width), flat(half // cut, width), whole(ff_own)]
        + [whole(own)] * 8,
        out_shape=[shape((own, 3 * width), F32), shape((own, width), F32), shape((own, ff), F32),
                   shape((ff_own, width), F32), shape((half, width)), shape((ff_own,), F32)]
        + [shape((own,), F32)] * 8,
        compiler_params=pltpu.CompilerParams(vmem_limit_bytes=VMEM_LIMIT),
    )(res.reshape(4, 2, own, own), res, got.reshape(3, own, own), gup, gfar, gdn, dkeep, drecv, total, ubias, dbias)
    return (
        out[None], gtok[None], gqkv, sums[0], sums[1], gout, sums[2], sums[3], sums[4], gup, ub, gdn, db,
        sums[5], sums[6],
    )


def solution(mesh):
    specs = dict(
        in_specs=(
            P("batch", "seq", None), P("seq", None), P(), P(), P("seq", None), P(), P(), P(),
            P("seq", None), P(), P("seq", None), P(), P(), P(), P("batch"), P("batch", None),
            P("batch"), P("batch", None, None),
        ),
        out_specs=(
            P("batch", "seq", None), P("batch", "seq", None), P("seq", None), P("seq"), P("seq"),
            P("seq", None), P("seq"), P("seq"), P("seq"), P("seq", None), P("seq"),
            P("seq", None), P("seq"), P("seq"), P("seq"),
        ),
    )
    return jax.shard_map(functools.partial(body, mesh), mesh=mesh, check_vma=False, **specs)
```
